128 devices in a mesh: row: 8 (over x, core), col: 16 (over y, z).
Axes of the slice: x: 4, y: 4, z: 4, core: 2. Of those that a mesh axis runs over, the one named last changes fastest.
Arguments:
- density_factor: bfloat16 [524288, 256], P(('row', 'col'))
- onsite: float32 [524288], P(('row', 'col')), may hold values from -4 to 4
- neighbour_ids: int32 [1024, 8], P(('row', 'col')), may hold values from 0 to 1023, as said below
- neighbour_count: int32 [1024], P(('row', 'col')), may hold values from 1 to 8, as said below
- coupling_type: int32 [1024, 8], P(('row', 'col')), may hold values from 0 to 3
- coupling_blocks: bfloat16 [4, 512, 512], replicated, may hold values from -0.25 to 0.25
- bath_pattern: int32 [1024], P(('row', 'col')), may hold values from 0 to 3
- bath_blocks: bfloat16 [4, 512, 512], replicated, may hold values from -0.25 to 0.25
Outputs:
- new_factor: bfloat16 [524288, 256], P(('row', 'col'))
The draws below stay inside these ranges and needn't reach their ends.
Inputs may be any that keep to these rules, and one draw needn't show every extreme that they name: `neighbour_ids`: every neighbour of block b lies among the 128 blocks that share b's index of row, at most half of 128 blocks from b when that group is taken as a loop, and is never b itself; some block has a neighbour exactly half of 128 blocks away. Only the first neighbour_count[b] slots of block b's lists are used; some block uses all 8.
All inputs are finite; a program needn't handle non-finite values.
Results may differ from the reference program's by a relative error of at most 0.0056.
Values may be sent and summed in bfloat16 or wider, within the bound.
A program may use at most 192 MiB of HBM per device.

```python
import jax
import jax.numpy as jnp
from jax import lax

BLK = 512
RANK = 256
NT = 4
NB = 4
KMAX = 8
SWEEPS = 2
NBLK = 1024
NST = 524288
GROUP = 128


def draw_density_factor(key, part):
    keys = jax.random.split(key, 3)
    positions = jnp.arange(NST, dtype=jnp.float32)[:, None]
    rising = 1.0 + 2.0 * positions / NST
    row_scale = jnp.exp(jax.random.uniform(keys[1], (NST, 1), jnp.float32) * jnp.log(10.0))
    col_scale = jnp.exp(jax.random.uniform(keys[2], (1, RANK), jnp.float32) * jnp.log(3.0))
    values = jnp.clip(jax.random.normal(keys[0], (NST, RANK), jnp.float32), -6.0, 6.0)
    return (values * row_scale * col_scale * rising * 0.125).astype(jnp.bfloat16)


def draw_neighbour_ids(key, part):
    first_key, second_key = jax.random.split(key)
    blocks = jnp.arange(NBLK, dtype=jnp.int32)[:, None]
    reach = GROUP // 2
    distance = jax.random.randint(first_key, (NBLK, KMAX), 1, reach + 1)
    direction = jax.random.randint(second_key, (NBLK, KMAX), 0, 2) * 2 - 1
    offset = (distance * direction).at[0, 0].set(reach)
    group_start = blocks // GROUP * GROUP
    return (group_start + (blocks - group_start + offset) % GROUP).astype(jnp.int32)


def draw_neighbour_count(key, part):
    counts = jax.random.randint(key, (NBLK,), 1, KMAX + 1)
    return counts.at[0].set(KMAX).astype(jnp.int32)


def plant(values, own_key, smallest, largest):
    dims = values.shape
    spot = [jax.random.randint(jax.random.fold_in(own_key, axis), (), 0, dims[axis]) for axis in range(len(dims))]
    values = values.at[tuple(spot)].set(smallest)
    longest = dims.index(max(dims))
    spot[longest] = (spot[longest] + 1) % dims[longest]
    return values.at[tuple(spot)].set(largest)


def level_of(stream_key, dims, shards, low, top_value):
    factor_of, own = 1.0, jax.random.fold_in(stream_key, 6)
    for dim, blocks in shards:
        heights = jnp.exp(jax.random.uniform(jax.random.fold_in(own, dim), (blocks,), jnp.float32, low / len(shards), top_value / len(shards)))
        factor_of = factor_of * jnp.repeat(heights, dims[dim] // blocks).reshape([-1 if axis == dim else 1 for axis in range(len(dims))])
    return factor_of


def gaussian(rng, extent, spread, bound, cuts=(), kind=jnp.bfloat16):
    factor_of = level_of(rng, extent, cuts, -0.22, 0.18) if cuts else 1.0
    result = jax.random.normal(rng, extent, jnp.float32) * spread * factor_of
    return jnp.minimum(jnp.maximum(result, -bound), bound).astype(kind)


def setup_inputs(seed: int = 0) -> dict:
    seeds = jax.random.split(jax.random.key(seed), 9)
    return {
        "density_factor": draw_density_factor(jax.random.fold_in(seeds[8], 71), 0),
        "onsite": gaussian(seeds[1], (NST,), 1.0, 4.0, ((0, 128),), jnp.float32),
        "neighbour_ids": draw_neighbour_ids(jax.random.fold_in(seeds[8], 71), 0),
        "neighbour_count": draw_neighbour_count(jax.random.fold_in(seeds[8], 71), 0),
        "coupling_type": plant(jax.random.randint(seeds[4], (NBLK, KMAX), 0, NT), jax.random.fold_in(seeds[4], 1), 0, NT - 1).astype(jnp.int32),
        "coupling_blocks": gaussian(seeds[5], (NT, BLK, BLK), BLK ** -0.5, 0.25),
        "bath_pattern": plant(jax.random.randint(seeds[6], (NBLK,), 0, NB), jax.random.fold_in(seeds[6], 1), 0, NB - 1).astype(jnp.int32),
        "bath_blocks": gaussian(seeds[7], (NB, BLK, BLK), BLK ** -0.5, 0.25),
    }


time_step = 0.25

def orthonormal_steps(gram):
    basis = jnp.eye(2 * RANK, RANK, dtype=jnp.float32)
    for sweep in range(SWEEPS):
        image = jnp.dot(gram, basis, precision=lax.Precision.HIGHEST)
        inner = jnp.dot(image.T, image, precision=lax.Precision.HIGHEST)
        factor = jnp.linalg.cholesky(inner)
        basis = lax.linalg.triangular_solve(factor, image, left_side=False, lower=True, transpose_a=True)
    return basis

def reference(density_factor, onsite, neighbour_ids, neighbour_count, coupling_type, coupling_blocks, bath_pattern, bath_blocks):
    row_blocks = density_factor.reshape(NBLK, BLK, RANK)
    slot_index = jnp.arange(KMAX, dtype=jnp.int32)
    kind_index = jnp.arange(NT, dtype=jnp.int32)
    coupling_wide = coupling_blocks.astype(jnp.float32)

    def one_block(items):
        ids, count, kinds, bath_kind, own_rows = items
        slot_live = (slot_index < count).astype(jnp.float32)
        weights = (kinds[:, None] == kind_index[None, :]).astype(jnp.float32) * slot_live[:, None]
        fetched = row_blocks[ids].astype(jnp.float32)
        summed = jnp.einsum('kt,kir->tir', weights, fetched).astype(jnp.bfloat16)
        coupled = jnp.einsum('tij,tjr->ir', coupling_wide, summed.astype(jnp.float32))
        bathed = jnp.dot(bath_blocks[bath_kind].astype(jnp.float32), own_rows.astype(jnp.float32), preferred_element_type=jnp.float32).astype(jnp.bfloat16)
        return (coupled, bathed)
    coupled, bathed = lax.map(one_block, (neighbour_ids, neighbour_count, coupling_type, bath_pattern, row_blocks))
    coupled = coupled.reshape(NST, RANK)
    bathed = bathed.reshape(NST, RANK)
    factor_wide = density_factor.astype(jnp.float32)
    moved = (factor_wide - time_step * (onsite[:, None] * factor_wide + coupled)).astype(jnp.bfloat16)
    stacked = jnp.concatenate([moved, bathed], axis=1)
    gram = lax.dot_general(stacked.astype(jnp.float32), stacked.astype(jnp.float32), (((0,), (0,)), ((), ())), preferred_element_type=jnp.float32)
    rotation = orthonormal_steps(gram).astype(jnp.bfloat16)
    return jnp.dot(stacked.astype(jnp.float32), rotation.astype(jnp.float32), preferred_element_type=jnp.float32).astype(jnp.bfloat16)
```

```python
import functools

import jax
import jax.numpy as jnp
from jax import lax
from jax.experimental import pallas as pl
from jax.experimental.pallas import tpu as pltpu
from jax.sharding import PartitionSpec as P

SWEEPS = 2


time_step = 0.25


def orthonormal_steps(gram, rank_cols):
    basis = jnp.eye(2 * rank_cols, rank_cols, dtype=jnp.float32)
    for sweep in range(SWEEPS):
        image = jnp.dot(gram, basis, precision=lax.Precision.HIGHEST)
        inner = jnp.dot(image.T, image, precision=lax.Precision.HIGHEST)
        factor = jnp.linalg.cholesky(inner)
        basis = lax.linalg.triangular_solve(
            factor, image, left_side=False, lower=True, transpose_a=True
        )
    return basis


def step_kernel(slots, ids_ref, cnt_ref, kind_ref, bath_ref,
                nbr_ref, own_ref, ons_ref, cpl_ref, bth_ref, out_ref, acc):
    b = pl.program_id(0)
    k = pl.program_id(1)
    rank_cols = own_ref.shape[2]

    @pl.when(k == 0)
    def _():
        acc[...] = jnp.zeros_like(acc)

    @pl.when(k < cnt_ref[b])
    def _():
        t = kind_ref[b * slots + k]
        acc[t] += nbr_ref[0].astype(jnp.float32)

    @pl.when(k == slots - 1)
    def _():
        coupled = jnp.dot(cpl_ref[0], acc[0].astype(jnp.bfloat16), preferred_element_type=jnp.float32)
        for t in range(1, cpl_ref.shape[0]):
            coupled += jnp.dot(cpl_ref[t], acc[t].astype(jnp.bfloat16), preferred_element_type=jnp.float32)
        own = own_ref[0]
        wide = own.astype(jnp.float32)
        moved = wide - time_step * (ons_ref[0] * wide + coupled)
        out_ref[0, :, :rank_cols] = moved.astype(out_ref.dtype)
        bathed = jnp.dot(bth_ref[0], own, preferred_element_type=jnp.float32)
        out_ref[0, :, rank_cols:] = bathed.astype(out_ref.dtype)


def stacked_blocks(group_rows, own_rows, energy, ids, counts, kinds, bath_pattern, coupling_blocks, bath_blocks):
    blocks, block_rows, rank_cols = own_rows.shape
    slots = ids.shape[0] // blocks
    kinds_n = coupling_blocks.shape[0]

    def nbr_map(b, k, ids_ref, cnt_ref, kind_ref, bath_ref):
        live = jnp.minimum(k, cnt_ref[b] - 1)
        return (ids_ref[b * slots + live], 0, 0)

    grid_spec = pltpu.PrefetchScalarGridSpec(
        num_scalar_prefetch=4,
        grid=(blocks, slots),
        in_specs=[
            pl.BlockSpec((1, block_rows, rank_cols), nbr_map),
            pl.BlockSpec((1, block_rows, rank_cols), lambda b, k, *_: (b, 0, 0)),
            pl.BlockSpec((1, block_rows, 1), lambda b, k, *_: (b, 0, 0)),
            pl.BlockSpec((kinds_n, block_rows, block_rows), lambda b, k, *_: (0, 0, 0)),
            pl.BlockSpec((1, block_rows, block_rows), lambda b, k, i, c, t, bp: (bp[b], 0, 0)),
        ],
        out_specs=pl.BlockSpec((1, block_rows, 2 * rank_cols), lambda b, k, *_: (b, 0, 0)),
        scratch_shapes=[pltpu.VMEM((kinds_n, block_rows, rank_cols), jnp.float32)],
    )
    return pl.pallas_call(
        functools.partial(step_kernel, slots),
        grid_spec=grid_spec,
        out_shape=jax.ShapeDtypeStruct((blocks, block_rows, 2 * rank_cols), jnp.bfloat16),
    )(ids, counts, kinds, bath_pattern, group_rows, own_rows, energy, coupling_blocks, bath_blocks)


def halving_sum(local, axes, count):
    me = lax.axis_index(axes)
    buf = local.reshape(-1)
    stages = []
    order = [s for s in range(count.bit_length() - 1)]
    for s in order:
        bit = (me >> s) & 1
        half = buf.shape[0] // 2
        low, high = buf[:half], buf[half:]
        send = jnp.where(bit == 1, low, high)
        keep = jnp.where(bit == 1, high, low)
        pairs = [(i, i ^ (1 << s)) for i in range(count)]
        buf = keep + lax.ppermute(send, axes, pairs)
        stages.append((s, bit))
    for s, bit in reversed(stages):
        pairs = [(i, i ^ (1 << s)) for i in range(count)]
        other = lax.ppermute(buf, axes, pairs)
        buf = jnp.where(bit == 1, jnp.concatenate([other, buf]), jnp.concatenate([buf, other]))
    return buf.reshape(local.shape)


def shards(
    density_factor,
    onsite,
    neighbour_ids,
    neighbour_count,
    coupling_type,
    coupling_blocks,
    bath_pattern,
    bath_blocks,
):
    blocks, slots = neighbour_ids.shape
    block_rows = coupling_blocks.shape[1]
    rank_cols = density_factor.shape[1]
    col_count = lax.axis_size("col")
    group_blocks = col_count * blocks
    row_place = lax.axis_index("row")
    in_group = jnp.clip(neighbour_ids - row_place * group_blocks, 0, group_blocks - 1)
    counts = jnp.clip(neighbour_count, 1, slots)
    kinds = jnp.clip(coupling_type, 0, coupling_blocks.shape[0] - 1)
    bath_kind = jnp.clip(bath_pattern, 0, bath_blocks.shape[0] - 1)
    gathered = lax.all_gather(density_factor, "col", axis=0, tiled=True)
    group_rows = gathered.reshape(group_blocks, block_rows, rank_cols)
    own_rows = density_factor.reshape(blocks, block_rows, rank_cols)
    energy = onsite.reshape(blocks, block_rows, 1)
    stacked = stacked_blocks(
        group_rows, own_rows, energy, in_group.reshape(-1), counts, kinds.reshape(-1), bath_kind,
        coupling_blocks, bath_blocks,
    ).reshape(blocks * block_rows, 2 * rank_cols)
    local_gram = lax.dot_general(
        stacked, stacked, (((0,), (0,)), ((), ())), preferred_element_type=jnp.float32
    )
    devices = lax.axis_size("row") * col_count
    gram_sum = halving_sum(local_gram, ("row", "col"), devices)
    rotation = orthonormal_steps(gram_sum, rank_cols).astype(jnp.bfloat16)
    return jnp.dot(stacked, rotation, preferred_element_type=jnp.float32).astype(jnp.bfloat16)


def solution(mesh):
    placed = (
        P(("row", "col"), None),
        P(("row", "col")),
        P(("row", "col"), None),
        P(("row", "col")),
        P(("row", "col"), None),
        P(),
        P(("row", "col")),
        P(),
    )
    return jax.shard_map(
        shards, mesh=mesh, in_specs=placed, out_specs=P(("row", "col"), None), check_vma=False
    )
```

```python
import functools

import jax
import jax.numpy as jnp
from jax import lax
from jax.experimental import pallas as pl
from jax.experimental.pallas import tpu as pltpu
from jax.sharding import PartitionSpec as P

SWEEPS = 2


time_step = 0.25


def orthonormal_steps(gram, rank_cols):
    basis = jnp.eye(2 * rank_cols, rank_cols, dtype=jnp.float32)
    for sweep in range(SWEEPS):
        image = jnp.dot(gram, basis, precision=lax.Precision.HIGHEST)
        inner = jnp.dot(image.T, image, precision=lax.Precision.HIGHEST)
        factor = jnp.linalg.cholesky(inner)
        basis = lax.linalg.triangular_solve(
            factor, image, left_side=False, lower=True, transpose_a=True
        )
    return basis


def step_kernel(slots, ids_ref, cnt_ref, kind_ref, bath_ref,
                group_hbm, own_ref, ons_ref, cpl_ref, bth_ref, out_ref, buf, sems, acc):
    b = pl.program_id(0)
    last = pl.num_programs(0) - 1
    rank_cols = own_ref.shape[2]

    def fetch(blk, slot):
        for k in range(slots):
            @pl.when(k < cnt_ref[blk])
            def _():
                pltpu.make_async_copy(
                    group_hbm.at[ids_ref[blk * slots + k]], buf.at[slot, k], sems.at[slot, k]
                ).start()

    @pl.when(b == 0)
    def _():
        fetch(0, 0)

    @pl.when(b < last)
    def _():
        fetch(b + 1, (b + 1) % 2)

    slot = b % 2
    acc[...] = jnp.zeros_like(acc)
    for k in range(slots):
        @pl.when(k < cnt_ref[b])
        def _():
            pltpu.make_async_copy(group_hbm.at[0], buf.at[slot, k], sems.at[slot, k]).wait()
            t = kind_ref[b * slots + k]
            acc[t] += buf[slot, k].astype(jnp.float32)

    coupled = jnp.dot(cpl_ref[0], acc[0].astype(jnp.bfloat16), preferred_element_type=jnp.float32)
    for t in range(1, cpl_ref.shape[0]):
        coupled += jnp.dot(cpl_ref[t], acc[t].astype(jnp.bfloat16), preferred_element_type=jnp.float32)
    own = own_ref[0]
    wide = own.astype(jnp.float32)
    moved = wide - time_step * (ons_ref[0] * wide + coupled)
    out_ref[0, :, :rank_cols] = moved.astype(out_ref.dtype)
    bathed = jnp.dot(bth_ref[0], own, preferred_element_type=jnp.float32)
    out_ref[0, :, rank_cols:] = bathed.astype(out_ref.dtype)


def stacked_blocks(group_rows, own_rows, energy, ids, counts, kinds, bath_pattern, coupling_blocks, bath_blocks):
    blocks, block_rows, rank_cols = own_rows.shape
    slots = ids.shape[0] // blocks
    kinds_n = coupling_blocks.shape[0]
    grid_spec = pltpu.PrefetchScalarGridSpec(
        num_scalar_prefetch=4,
        grid=(blocks,),
        in_specs=[
            pl.BlockSpec(memory_space=pl.ANY),
            pl.BlockSpec((1, block_rows, rank_cols), lambda b, *_: (b, 0, 0)),
            pl.BlockSpec((1, block_rows, 1), lambda b, *_: (b, 0, 0)),
            pl.BlockSpec((kinds_n, block_rows, block_rows), lambda b, *_: (0, 0, 0)),
            pl.BlockSpec((1, block_rows, block_rows), lambda b, i, c, t, bp: (bp[b], 0, 0)),
        ],
        out_specs=pl.BlockSpec((1, block_rows, 2 * rank_cols), lambda b, *_: (b, 0, 0)),
        scratch_shapes=[
            pltpu.VMEM((2, slots, block_rows, rank_cols), group_rows.dtype),
            pltpu.SemaphoreType.DMA((2, slots)),
            pltpu.VMEM((kinds_n, block_rows, rank_cols), jnp.float32),
        ],
    )
    return pl.pallas_call(
        functools.partial(step_kernel, slots),
        grid_spec=grid_spec,
        out_shape=jax.ShapeDtypeStruct((blocks, block_rows, 2 * rank_cols), jnp.bfloat16),
        compiler_params=pltpu.CompilerParams(dimension_semantics=("arbitrary",)),
    )(ids, counts, kinds, bath_pattern, group_rows, own_rows, energy, coupling_blocks, bath_blocks)


def pack_symmetric(gram, half):
    upper = gram[:half, half:]
    rows = lax.broadcasted_iota(jnp.int32, (half, half), 0)
    cols = lax.broadcasted_iota(jnp.int32, (half, half), 1)
    corner = gram[half:, half:]
    mixed = jnp.where(rows <= cols, gram[:half, :half], corner)
    return jnp.concatenate([upper.reshape(-1), mixed.reshape(-1), jnp.diagonal(corner)])


def unpack_symmetric(packed, half):
    area = half * half
    upper = packed[:area].reshape(half, half)
    mixed = packed[area:2 * area].reshape(half, half)
    diag = packed[2 * area:]
    rows = lax.broadcasted_iota(jnp.int32, (half, half), 0)
    cols = lax.broadcasted_iota(jnp.int32, (half, half), 1)
    first = jnp.where(rows <= cols, mixed, mixed.T)
    corner = jnp.where(rows > cols, mixed, mixed.T)
    corner = jnp.where(rows == cols, diag[None, :], corner)
    return jnp.concatenate(
        [jnp.concatenate([first, upper], axis=1), jnp.concatenate([upper.T, corner], axis=1)], axis=0
    )


def halving_sum(local, axes, count, order):
    me = lax.axis_index(axes)
    buf = local
    stages = []
    for s in order:
        bit = (me >> s) & 1
        half = buf.shape[0] // 2
        low, high = buf[:half], buf[half:]
        send = jnp.where(bit == 1, low, high)
        keep = jnp.where(bit == 1, high, low)
        pairs = [(i, i ^ (1 << s)) for i in range(count)]
        buf = keep + lax.ppermute(send, axes, pairs)
        stages.append((s, bit))
    for s, bit in reversed(stages):
        pairs = [(i, i ^ (1 << s)) for i in range(count)]
        other = lax.ppermute(buf, axes, pairs)
        buf = jnp.where(bit == 1, jnp.concatenate([other, buf]), jnp.concatenate([buf, other]))
    return buf


def shards(
    density_factor,
    onsite,
    neighbour_ids,
    neighbour_count,
    coupling_type,
    coupling_blocks,
    bath_pattern,
    bath_blocks,
):
    blocks, slots = neighbour_ids.shape
    block_rows = coupling_blocks.shape[1]
    rank_cols = density_factor.shape[1]
    col_count = lax.axis_size("col")
    group_blocks = col_count * blocks
    row_place = lax.axis_index("row")
    in_group = jnp.clip(neighbour_ids - row_place * group_blocks, 0, group_blocks - 1)
    counts = jnp.clip(neighbour_count, 1, slots)
    kinds = jnp.clip(coupling_type, 0, coupling_blocks.shape[0] - 1)
    bath_kind = jnp.clip(bath_pattern, 0, bath_blocks.shape[0] - 1)
    gathered = lax.all_gather(density_factor, "col", axis=0, tiled=True)
    group_rows = gathered.reshape(group_blocks, block_rows, rank_cols)
    own_rows = density_factor.reshape(blocks, block_rows, rank_cols)
    energy = onsite.reshape(blocks, block_rows, 1)
    stacked = stacked_blocks(
        group_rows, own_rows, energy, in_group.reshape(-1), counts, kinds.reshape(-1), bath_kind,
        coupling_blocks, bath_blocks,
    ).reshape(blocks * block_rows, 2 * rank_cols)
    local_gram = lax.dot_general(
        stacked, stacked, (((0,), (0,)), ((), ())), preferred_element_type=jnp.float32
    )
    devices = lax.axis_size("row") * col_count
    stage_bits = devices.bit_length() - 1
    order = [4, 0, 2, 5, 1, 3, 6] if stage_bits == 7 else list(range(stage_bits))
    packed = halving_sum(pack_symmetric(local_gram, rank_cols), ("row", "col"), devices, order)
    gram_sum = unpack_symmetric(packed, rank_cols)
    rotation = orthonormal_steps(gram_sum, rank_cols).astype(jnp.bfloat16)
    return jnp.dot(stacked, rotation, preferred_element_type=jnp.float32).astype(jnp.bfloat16)


def solution(mesh):
    placed = (
        P(("row", "col"), None),
        P(("row", "col")),
        P(("row", "col"), None),
        P(("row", "col")),
        P(("row", "col"), None),
        P(),
        P(("row", "col")),
        P(),
    )
    return jax.shard_map(
        shards, mesh=mesh, in_specs=placed, out_specs=P(("row", "col"), None), check_vma=False
    )
```

```python
import functools

import jax
import jax.numpy as jnp
from jax import lax
from jax.experimental import pallas as pl
from jax.experimental.pallas import tpu as pltpu
from jax.sharding import PartitionSpec as P

SWEEPS = 2


time_step = 0.25


def orthonormal_steps(gram, rank_cols):
    def sweep(_, basis):
        image = jnp.dot(gram, basis, precision=lax.Precision.HIGHEST)
        inner = jnp.dot(image.T, image, precision=lax.Precision.HIGHEST)
        factor = jnp.linalg.cholesky(inner)
        return lax.linalg.triangular_solve(
            factor, image, left_side=False, lower=True, transpose_a=True
        )

    return lax.fori_loop(0, SWEEPS, sweep, jnp.eye(2 * rank_cols, rank_cols, dtype=jnp.float32))


def step_kernel(slots, ids_ref, cnt_ref, kind_ref, bath_ref,
                group_hbm, own_ref, ons_ref, cpl_ref, bth_ref, out_ref, buf, sems, acc):
    b = pl.program_id(0)
    last = pl.num_programs(0) - 1
    rank_cols = own_ref.shape[2]

    def fetch(blk, slot):
        for k in range(slots):
            @pl.when(k < cnt_ref[blk])
            def _():
                pltpu.make_async_copy(
                    group_hbm.at[ids_ref[blk * slots + k]], buf.at[slot, k], sems.at[slot, k]
                ).start()

    @pl.when(b == 0)
    def _():
        fetch(0, 0)

    @pl.when(b < last)
    def _():
        fetch(b + 1, (b + 1) % 2)

    slot = b % 2
    acc[...] = jnp.zeros_like(acc)
    for k in range(slots):
        @pl.when(k < cnt_ref[b])
        def _():
            pltpu.make_async_copy(group_hbm.at[0], buf.at[slot, k], sems.at[slot, k]).wait()
            t = kind_ref[b * slots + k]
            acc[t] += buf[slot, k].astype(jnp.float32)

    coupled = jnp.dot(cpl_ref[0], acc[0].astype(jnp.bfloat16), preferred_element_type=jnp.float32)
    for t in range(1, cpl_ref.shape[0]):
        coupled += jnp.dot(cpl_ref[t], acc[t].astype(jnp.bfloat16), preferred_element_type=jnp.float32)
    own = own_ref[0]
    wide = own.astype(jnp.float32)
    moved = wide - time_step * (ons_ref[0] * wide + coupled)
    out_ref[0, :, :rank_cols] = moved.astype(out_ref.dtype)
    bathed = jnp.dot(bth_ref[0], own, preferred_element_type=jnp.float32)
    out_ref[0, :, rank_cols:] = bathed.astype(out_ref.dtype)


def stacked_blocks(group_rows, own_rows, energy, ids, counts, kinds, bath_pattern, coupling_blocks, bath_blocks):
    blocks, block_rows, rank_cols = own_rows.shape
    slots = ids.shape[0] // blocks
    kinds_n = coupling_blocks.shape[0]
    grid_spec = pltpu.PrefetchScalarGridSpec(
        num_scalar_prefetch=4,
        grid=(blocks,),
        in_specs=[
            pl.BlockSpec(memory_space=pl.ANY),
            pl.BlockSpec((1, block_rows, rank_cols), lambda b, *_: (b, 0, 0)),
            pl.BlockSpec((1, block_rows, 1), lambda b, *_: (b, 0, 0)),
            pl.BlockSpec((kinds_n, block_rows, block_rows), lambda b, *_: (0, 0, 0)),
            pl.BlockSpec((1, block_rows, block_rows), lambda b, i, c, t, bp: (bp[b], 0, 0)),
        ],
        out_specs=pl.BlockSpec((1, block_rows, 2 * rank_cols), lambda b, *_: (b, 0, 0)),
        scratch_shapes=[
            pltpu.VMEM((2, slots, block_rows, rank_cols), group_rows.dtype),
            pltpu.SemaphoreType.DMA((2, slots)),
            pltpu.VMEM((kinds_n, block_rows, rank_cols), jnp.float32),
        ],
    )
    return pl.pallas_call(
        functools.partial(step_kernel, slots),
        grid_spec=grid_spec,
        out_shape=jax.ShapeDtypeStruct((blocks, block_rows, 2 * rank_cols), jnp.bfloat16),
        compiler_params=pltpu.CompilerParams(dimension_semantics=("arbitrary",)),
    )(ids, counts, kinds, bath_pattern, group_rows, own_rows, energy, coupling_blocks, bath_blocks)


def pack_symmetric(gram, half):
    upper = gram[:half, half:]
    rows = lax.broadcasted_iota(jnp.int32, (half, half), 0)
    cols = lax.broadcasted_iota(jnp.int32, (half, half), 1)
    corner = gram[half:, half:]
    mixed = jnp.where(rows <= cols, gram[:half, :half], corner)
    return jnp.concatenate([upper.reshape(-1), mixed.reshape(-1), jnp.diagonal(corner)])


def unpack_symmetric(packed, half):
    area = half * half
    upper = packed[:area].reshape(half, half)
    mixed = packed[area:2 * area].reshape(half, half)
    diag = packed[2 * area:]
    rows = lax.broadcasted_iota(jnp.int32, (half, half), 0)
    cols = lax.broadcasted_iota(jnp.int32, (half, half), 1)
    first = jnp.where(rows <= cols, mixed, mixed.T)
    corner = jnp.where(rows > cols, mixed, mixed.T)
    corner = jnp.where(rows == cols, diag[None, :], corner)
    return jnp.concatenate(
        [jnp.concatenate([first, upper], axis=1), jnp.concatenate([upper.T, corner], axis=1)], axis=0
    )


def halving_sum(local, axes, count, order):
    me = lax.axis_index(axes)
    buf = local
    stages = []
    for s in order:
        bit = (me >> s) & 1
        half = buf.shape[0] // 2
        low, high = buf[:half], buf[half:]
        send = jnp.where(bit == 1, low, high)
        keep = jnp.where(bit == 1, high, low)
        pairs = [(i, i ^ (1 << s)) for i in range(count)]
        buf = keep + lax.ppermute(send, axes, pairs)
        stages.append((s, bit))
    for s, bit in reversed(stages):
        pairs = [(i, i ^ (1 << s)) for i in range(count)]
        other = lax.ppermute(buf, axes, pairs)
        buf = jnp.where(bit == 1, jnp.concatenate([other, buf]), jnp.concatenate([buf, other]))
    return buf


def shards(
    density_factor,
    onsite,
    neighbour_ids,
    neighbour_count,
    coupling_type,
    coupling_blocks,
    bath_pattern,
    bath_blocks,
):
    blocks, slots = neighbour_ids.shape
    block_rows = coupling_blocks.shape[1]
    rank_cols = density_factor.shape[1]
    col_count = lax.axis_size("col")
    group_blocks = col_count * blocks
    row_place = lax.axis_index("row")
    in_group = jnp.clip(neighbour_ids - row_place * group_blocks, 0, group_blocks - 1)
    counts = jnp.clip(neighbour_count, 1, slots)
    kinds = jnp.clip(coupling_type, 0, coupling_blocks.shape[0] - 1)
    bath_kind = jnp.clip(bath_pattern, 0, bath_blocks.shape[0] - 1)
    gathered = lax.all_gather(density_factor, "col", axis=0, tiled=True)
    group_rows = gathered.reshape(group_blocks, block_rows, rank_cols)
    own_rows = density_factor.reshape(blocks, block_rows, rank_cols)
    energy = onsite.reshape(blocks, block_rows, 1)
    stacked = stacked_blocks(
        group_rows, own_rows, energy, in_group.reshape(-1), counts, kinds.reshape(-1), bath_kind,
        coupling_blocks, bath_blocks,
    ).reshape(blocks * block_rows, 2 * rank_cols)
    local_gram = lax.dot_general(
        stacked, stacked, (((0,), (0,)), ((), ())), preferred_element_type=jnp.float32
    )
    devices = lax.axis_size("row") * col_count
    stage_bits = devices.bit_length() - 1
    order = [4, 0, 2, 5, 1, 3, 6] if stage_bits == 7 else list(range(stage_bits))
    packed = halving_sum(pack_symmetric(local_gram, rank_cols), ("row", "col"), devices, order)
    gram_sum = unpack_symmetric(packed, rank_cols)
    rotation = orthonormal_steps(gram_sum, rank_cols).astype(jnp.bfloat16)
    return jnp.dot(stacked, rotation, preferred_element_type=jnp.float32).astype(jnp.bfloat16)


def solution(mesh):
    placed = (
        P(("row", "col"), None),
        P(("row", "col")),
        P(("row", "col"), None),
        P(("row", "col")),
        P(("row", "col"), None),
        P(),
        P(("row", "col")),
        P(),
    )
    return jax.shard_map(
        shards, mesh=mesh, in_specs=placed, out_specs=P(("row", "col"), None), check_vma=False
    )
```

```python
import functools

import jax
import jax.numpy as jnp
from jax import lax
from jax.experimental import pallas as pl
from jax.experimental.pallas import tpu as pltpu
from jax.sharding import PartitionSpec as P

SWEEPS = 2


time_step = 0.25


def orthonormal_steps(gram, rank_cols):
    def sweep(_, basis):
        image = jnp.dot(gram, basis, precision=lax.Precision.HIGHEST)
        inner = jnp.dot(image.T, image, precision=lax.Precision.HIGHEST)
        factor = jnp.linalg.cholesky(inner)
        return lax.linalg.triangular_solve(
            factor, image, left_side=False, lower=True, transpose_a=True
        )

    return lax.fori_loop(0, SWEEPS, sweep, jnp.eye(2 * rank_cols, rank_cols, dtype=jnp.float32))


def step_kernel(slots, ids_ref, cnt_ref, kind_ref, bath_ref,
                group_hbm, own_ref, ons_ref, cpl_ref, bth_ref, out_ref, buf, sems, acc):
    b = pl.program_id(0)
    last = pl.num_programs(0) - 1
    rank_cols = own_ref.shape[2]

    def fetch(blk, slot):
        for k in range(slots):
            @pl.when(k < cnt_ref[blk])
            def _():
                pltpu.make_async_copy(
                    group_hbm.at[ids_ref[blk * slots + k]], buf.at[slot, k], sems.at[slot, k]
                ).start()

    @pl.when(b == 0)
    def _():
        fetch(0, 0)

    @pl.when(b < last)
    def _():
        fetch(b + 1, (b + 1) % 2)

    slot = b % 2
    acc[...] = jnp.zeros_like(acc)
    for k in range(slots):
        @pl.when(k < cnt_ref[b])
        def _():
            pltpu.make_async_copy(group_hbm.at[0], buf.at[slot, k], sems.at[slot, k]).wait()
            t = kind_ref[b * slots + k]
            acc[t] += buf[slot, k].astype(jnp.float32)

    coupled = jnp.dot(cpl_ref[0], acc[0].astype(jnp.bfloat16), preferred_element_type=jnp.float32)
    for t in range(1, cpl_ref.shape[0]):
        coupled += jnp.dot(cpl_ref[t], acc[t].astype(jnp.bfloat16), preferred_element_type=jnp.float32)
    own = own_ref[0]
    wide = own.astype(jnp.float32)
    moved = wide - time_step * (ons_ref[0] * wide + coupled)
    out_ref[0, :, :rank_cols] = moved.astype(out_ref.dtype)
    bathed = jnp.dot(bth_ref[0], own, preferred_element_type=jnp.float32)
    out_ref[0, :, rank_cols:] = bathed.astype(out_ref.dtype)


def stacked_blocks(group_rows, own_rows, energy, ids, counts, kinds, bath_pattern, coupling_blocks, bath_blocks):
    blocks, block_rows, rank_cols = own_rows.shape
    slots = ids.shape[0] // blocks
    kinds_n = coupling_blocks.shape[0]
    grid_spec = pltpu.PrefetchScalarGridSpec(
        num_scalar_prefetch=4,
        grid=(blocks,),
        in_specs=[
            pl.BlockSpec(memory_space=pl.ANY),
            pl.BlockSpec((1, block_rows, rank_cols), lambda b, *_: (b, 0, 0)),
            pl.BlockSpec((1, block_rows, 1), lambda b, *_: (b, 0, 0)),
            pl.BlockSpec((kinds_n, block_rows, block_rows), lambda b, *_: (0, 0, 0)),
            pl.BlockSpec((1, block_rows, block_rows), lambda b, i, c, t, bp: (bp[b], 0, 0)),
        ],
        out_specs=pl.BlockSpec((1, block_rows, 2 * rank_cols), lambda b, *_: (b, 0, 0)),
        scratch_shapes=[
            pltpu.VMEM((2, slots, block_rows, rank_cols), group_rows.dtype),
            pltpu.SemaphoreType.DMA((2, slots)),
            pltpu.VMEM((kinds_n, block_rows, rank_cols), jnp.float32),
        ],
    )
    return pl.pallas_call(
        functools.partial(step_kernel, slots),
        grid_spec=grid_spec,
        out_shape=jax.ShapeDtypeStruct((blocks, block_rows, 2 * rank_cols), jnp.bfloat16),
        compiler_params=pltpu.CompilerParams(dimension_semantics=("arbitrary",)),
    )(ids, counts, kinds, bath_pattern, group_rows, own_rows, energy, coupling_blocks, bath_blocks)


def allreduce_kernel(order, cols, x_ref, o_ref, *scratch):
    stages = len(order)
    recv_bufs = scratch[:stages]
    send_sems, recv_sems, work = scratch[stages], scratch[stages + 1], scratch[stages + 2]
    me = lax.axis_index("row") * cols + lax.axis_index("col")

    def bit(s):
        return (me // (1 << s)) % 2

    def place(s):
        other = me + (1 - 2 * bit(s)) * (1 << s)
        return (other // cols, other % cols)

    barrier = pltpu.get_barrier_semaphore()
    for s in order:
        pl.semaphore_signal(barrier, inc=1, device_id=place(s), device_id_type=pl.DeviceIdType.MESH)
    pl.semaphore_wait(barrier, stages)

    base = 0
    size = x_ref.shape[0]
    for j, s in enumerate(order):
        half = size // 2
        b = bit(s)
        keep = pl.multiple_of(base + b * half, 8)
        give = pl.multiple_of(base + (1 - b) * half, 8)
        src = x_ref if j == 0 else work
        copy = pltpu.make_async_remote_copy(
            src_ref=src.at[pl.ds(give, half)],
            dst_ref=recv_bufs[j],
            send_sem=send_sems.at[j],
            recv_sem=recv_sems.at[j],
            device_id=place(s),
            device_id_type=pl.DeviceIdType.MESH,
        )
        copy.start()
        copy.wait()
        work[pl.ds(keep, half)] = src[pl.ds(keep, half)] + recv_bufs[j][...]
        base, size = keep, half
    o_ref[pl.ds(base, size)] = work[pl.ds(base, size)]
    for j in reversed(range(stages)):
        s = order[j]
        block = o_ref.at[pl.ds(base, size)]
        copy = pltpu.make_async_remote_copy(
            src_ref=block,
            dst_ref=block,
            send_sem=send_sems.at[stages + j],
            recv_sem=recv_sems.at[stages + j],
            device_id=place(s),
            device_id_type=pl.DeviceIdType.MESH,
        )
        copy.start()
        copy.wait()
        base = pl.multiple_of(base - bit(s) * size, 8)
        size = size * 2


def kernel_sum(local, order, cols):
    lanes = 128
    flat = local.reshape(-1, lanes)
    rows = flat.shape[0]
    scratch = [pltpu.VMEM((rows >> (j + 1), lanes), jnp.float32) for j in range(len(order))]
    scratch += [pltpu.SemaphoreType.DMA((2 * len(order),)), pltpu.SemaphoreType.DMA((2 * len(order),))]
    scratch += [pltpu.VMEM(flat.shape, jnp.float32)]
    total = pl.pallas_call(
        functools.partial(allreduce_kernel, tuple(order), cols),
        out_shape=jax.ShapeDtypeStruct(flat.shape, flat.dtype),
        in_specs=[pl.BlockSpec(memory_space=pltpu.VMEM)],
        out_specs=pl.BlockSpec(memory_space=pltpu.VMEM),
        scratch_shapes=scratch,
        compiler_params=pltpu.CompilerParams(collective_id=0, has_side_effects=True),
    )(flat)
    return total.reshape(local.shape)


def shards(
    density_factor,
    onsite,
    neighbour_ids,
    neighbour_count,
    coupling_type,
    coupling_blocks,
    bath_pattern,
    bath_blocks,
):
    blocks, slots = neighbour_ids.shape
    block_rows = coupling_blocks.shape[1]
    rank_cols = density_factor.shape[1]
    col_count = lax.axis_size("col")
    group_blocks = col_count * blocks
    row_place = lax.axis_index("row")
    in_group = jnp.clip(neighbour_ids - row_place * group_blocks, 0, group_blocks - 1)
    counts = jnp.clip(neighbour_count, 1, slots)
    kinds = jnp.clip(coupling_type, 0, coupling_blocks.shape[0] - 1)
    bath_kind = jnp.clip(bath_pattern, 0, bath_blocks.shape[0] - 1)
    gathered = lax.all_gather(density_factor, "col", axis=0, tiled=True)
    group_rows = gathered.reshape(group_blocks, block_rows, rank_cols)
    own_rows = density_factor.reshape(blocks, block_rows, rank_cols)
    energy = onsite.reshape(blocks, block_rows, 1)
    stacked = stacked_blocks(
        group_rows, own_rows, energy, in_group.reshape(-1), counts, kinds.reshape(-1), bath_kind,
        coupling_blocks, bath_blocks,
    ).reshape(blocks * block_rows, 2 * rank_cols)
    local_gram = lax.dot_general(
        stacked, stacked, (((0,), (0,)), ((), ())), preferred_element_type=jnp.float32
    )
    devices = lax.axis_size("row") * col_count
    stage_bits = devices.bit_length() - 1
    order = [4, 0, 2, 5, 1, 3, 6] if stage_bits == 7 else list(range(stage_bits))
    gram_sum = kernel_sum(local_gram, order, col_count)
    rotation = orthonormal_steps(gram_sum, rank_cols).astype(jnp.bfloat16)
    return jnp.dot(stacked, rotation, preferred_element_type=jnp.float32).astype(jnp.bfloat16)


def solution(mesh):
    placed = (
        P(("row", "col"), None),
        P(("row", "col")),
        P(("row", "col"), None),
        P(("row", "col")),
        P(("row", "col"), None),
        P(),
        P(("row", "col")),
        P(),
    )
    return jax.shard_map(
        shards, mesh=mesh, in_specs=placed, out_specs=P(("row", "col"), None), check_vma=False
    )
```

```python
import functools

import jax
import jax.numpy as jnp
from jax import lax
from jax.experimental import pallas as pl
from jax.experimental.pallas import tpu as pltpu
from jax.sharding import PartitionSpec as P

SWEEPS = 2


time_step = 0.25


def orthonormal_steps(gram, rank_cols):
    def sweep(_, basis):
        image = jnp.dot(gram, basis, precision=lax.Precision.HIGHEST)
        inner = jnp.dot(image.T, image, precision=lax.Precision.HIGHEST)
        factor = jnp.linalg.cholesky(inner)
        return lax.linalg.triangular_solve(
            factor, image, left_side=False, lower=True, transpose_a=True
        )

    return lax.fori_loop(0, SWEEPS, sweep, jnp.eye(2 * rank_cols, rank_cols, dtype=jnp.float32))


def step_kernel(slots, ids_ref, cnt_ref, kind_ref, bath_ref,
                group_hbm, own_ref, ons_ref, cpl_ref, bth_ref, out_ref, buf, sems, acc):
    b = pl.program_id(0)
    last = pl.num_programs(0) - 1
    rank_cols = own_ref.shape[2]

    def fetch(blk, slot):
        for k in range(slots):
            @pl.when(k < cnt_ref[blk])
            def _():
                pltpu.make_async_copy(
                    group_hbm.at[ids_ref[blk * slots + k]], buf.at[slot, k], sems.at[slot, k]
                ).start()

    @pl.when(b == 0)
    def _():
        fetch(0, 0)

    @pl.when(b < last)
    def _():
        fetch(b + 1, (b + 1) % 2)

    slot = b % 2
    acc[...] = jnp.zeros_like(acc)
    for k in range(slots):
        @pl.when(k < cnt_ref[b])
        def _():
            pltpu.make_async_copy(group_hbm.at[0], buf.at[slot, k], sems.at[slot, k]).wait()
            t = kind_ref[b * slots + k]
            acc[t] += buf[slot, k].astype(jnp.float32)

    coupled = jnp.dot(cpl_ref[0], acc[0].astype(jnp.bfloat16), preferred_element_type=jnp.float32)
    for t in range(1, cpl_ref.shape[0]):
        coupled += jnp.dot(cpl_ref[t], acc[t].astype(jnp.bfloat16), preferred_element_type=jnp.float32)
    own = own_ref[0]
    wide = own.astype(jnp.float32)
    moved = wide - time_step * (ons_ref[0] * wide + coupled)
    out_ref[0, :, :rank_cols] = moved.astype(out_ref.dtype)
    bathed = jnp.dot(bth_ref[0], own, preferred_element_type=jnp.float32)
    out_ref[0, :, rank_cols:] = bathed.astype(out_ref.dtype)


def stacked_blocks(group_rows, own_rows, energy, ids, counts, kinds, bath_pattern, coupling_blocks, bath_blocks):
    blocks, block_rows, rank_cols = own_rows.shape
    slots = ids.shape[0] // blocks
    kinds_n = coupling_blocks.shape[0]
    grid_spec = pltpu.PrefetchScalarGridSpec(
        num_scalar_prefetch=4,
        grid=(blocks,),
        in_specs=[
            pl.BlockSpec(memory_space=pl.ANY),
            pl.BlockSpec((1, block_rows, rank_cols), lambda b, *_: (b, 0, 0)),
            pl.BlockSpec((1, block_rows, 1), lambda b, *_: (b, 0, 0)),
            pl.BlockSpec((kinds_n, block_rows, block_rows), lambda b, *_: (0, 0, 0)),
            pl.BlockSpec((1, block_rows, block_rows), lambda b, i, c, t, bp: (bp[b], 0, 0)),
        ],
        out_specs=pl.BlockSpec((1, block_rows, 2 * rank_cols), lambda b, *_: (b, 0, 0)),
        scratch_shapes=[
            pltpu.VMEM((2, slots, block_rows, rank_cols), group_rows.dtype),
            pltpu.SemaphoreType.DMA((2, slots)),
            pltpu.VMEM((kinds_n, block_rows, rank_cols), jnp.float32),
        ],
    )
    return pl.pallas_call(
        functools.partial(step_kernel, slots),
        grid_spec=grid_spec,
        out_shape=jax.ShapeDtypeStruct((blocks, block_rows, 2 * rank_cols), jnp.bfloat16),
        compiler_params=pltpu.CompilerParams(dimension_semantics=("arbitrary",)),
    )(ids, counts, kinds, bath_pattern, group_rows, own_rows, energy, coupling_blocks, bath_blocks)


def allreduce_kernel(fields, cols, x_ref, o_ref, *scratch):
    stages = len(fields)
    recv_bufs = scratch[:stages]
    send_sems, recv_sems, work = scratch[stages], scratch[stages + 1], scratch[stages + 2]
    me = lax.axis_index("row") * cols + lax.axis_index("col")

    def field(s, r):
        return (me // (1 << s)) % r

    def place(s, r, d):
        other = me + ((field(s, r) + d) % r - field(s, r)) * (1 << s)
        return (other // cols, other % cols)

    barrier = pltpu.get_barrier_semaphore()
    partners = 0
    for s, r in fields:
        for d in range(1, r):
            pl.semaphore_signal(barrier, inc=1, device_id=place(s, r, d), device_id_type=pl.DeviceIdType.MESH)
            partners += 1
    pl.semaphore_wait(barrier, partners)

    base = 0
    size = x_ref.shape[0]
    slot = 0
    for j, (s, r) in enumerate(fields):
        part = size // r
        f = field(s, r)
        src = x_ref if j == 0 else work
        copies = []
        for d in range(1, r):
            give = pl.multiple_of(base + ((f + d) % r) * part, 8)
            copy = pltpu.make_async_remote_copy(
                src_ref=src.at[pl.ds(give, part)],
                dst_ref=recv_bufs[j].at[d - 1],
                send_sem=send_sems.at[slot],
                recv_sem=recv_sems.at[slot],
                device_id=place(s, r, d),
                device_id_type=pl.DeviceIdType.MESH,
            )
            copy.start()
            copies.append(copy)
            slot += 1
        for copy in copies:
            copy.wait()
        keep = pl.multiple_of(base + f * part, 8)
        total = src[pl.ds(keep, part)]
        for d in range(1, r):
            total = total + recv_bufs[j][d - 1]
        work[pl.ds(keep, part)] = total
        base, size = keep, part
    o_ref[pl.ds(base, size)] = work[pl.ds(base, size)]
    for j in reversed(range(stages)):
        s, r = fields[j]
        block = o_ref.at[pl.ds(base, size)]
        copies = []
        for d in range(1, r):
            copy = pltpu.make_async_remote_copy(
                src_ref=block,
                dst_ref=block,
                send_sem=send_sems.at[slot],
                recv_sem=recv_sems.at[slot],
                device_id=place(s, r, d),
                device_id_type=pl.DeviceIdType.MESH,
            )
            copy.start()
            copies.append(copy)
            slot += 1
        for copy in copies:
            copy.wait()
        base = pl.multiple_of(base - field(s, r) * size, 8)
        size = size * r


def kernel_sum(local, fields, cols):
    lanes = 128
    flat = local.reshape(-1, lanes)
    rows = flat.shape[0]
    scratch = []
    left = rows
    for s, r in fields:
        left //= r
        scratch.append(pltpu.VMEM((r - 1, left, lanes), jnp.float32))
    copies = 2 * sum(r - 1 for _, r in fields)
    scratch += [pltpu.SemaphoreType.DMA((copies,)), pltpu.SemaphoreType.DMA((copies,))]
    scratch += [pltpu.VMEM(flat.shape, jnp.float32)]
    total = pl.pallas_call(
        functools.partial(allreduce_kernel, tuple(fields), cols),
        out_shape=jax.ShapeDtypeStruct(flat.shape, flat.dtype),
        in_specs=[pl.BlockSpec(memory_space=pltpu.VMEM)],
        out_specs=pl.BlockSpec(memory_space=pltpu.VMEM),
        scratch_shapes=scratch,
        compiler_params=pltpu.CompilerParams(collective_id=0, has_side_effects=True),
    )(flat)
    return total.reshape(local.shape)


def shards(
    density_factor,
    onsite,
    neighbour_ids,
    neighbour_count,
    coupling_type,
    coupling_blocks,
    bath_pattern,
    bath_blocks,
):
    blocks, slots = neighbour_ids.shape
    block_rows = coupling_blocks.shape[1]
    rank_cols = density_factor.shape[1]
    col_count = lax.axis_size("col")
    group_blocks = col_count * blocks
    row_place = lax.axis_index("row")
    in_group = jnp.clip(neighbour_ids - row_place * group_blocks, 0, group_blocks - 1)
    counts = jnp.clip(neighbour_count, 1, slots)
    kinds = jnp.clip(coupling_type, 0, coupling_blocks.shape[0] - 1)
    bath_kind = jnp.clip(bath_pattern, 0, bath_blocks.shape[0] - 1)
    gathered = lax.all_gather(density_factor, "col", axis=0, tiled=True)
    group_rows = gathered.reshape(group_blocks, block_rows, rank_cols)
    own_rows = density_factor.reshape(blocks, block_rows, rank_cols)
    energy = onsite.reshape(blocks, block_rows, 1)
    stacked = stacked_blocks(
        group_rows, own_rows, energy, in_group.reshape(-1), counts, kinds.reshape(-1), bath_kind,
        coupling_blocks, bath_blocks,
    ).reshape(blocks * block_rows, 2 * rank_cols)
    local_gram = lax.dot_general(
        stacked, stacked, (((0,), (0,)), ((), ())), preferred_element_type=jnp.float32
    )
    devices = lax.axis_size("row") * col_count
    stage_bits = devices.bit_length() - 1
    if stage_bits == 7:
        fields = [(4, 2), (0, 4), (2, 4), (5, 4)]
    else:
        fields = [(s, 2) for s in range(stage_bits)]
    gram_sum = kernel_sum(local_gram, fields, col_count)
    rotation = orthonormal_steps(gram_sum, rank_cols).astype(jnp.bfloat16)
    return jnp.dot(stacked, rotation, preferred_element_type=jnp.float32).astype(jnp.bfloat16)


def solution(mesh):
    placed = (
        P(("row", "col"), None),
        P(("row", "col")),
        P(("row", "col"), None),
        P(("row", "col")),
        P(("row", "col"), None),
        P(),
        P(("row", "col")),
        P(),
    )
    return jax.shard_map(
        shards, mesh=mesh, in_specs=placed, out_specs=P(("row", "col"), None), check_vma=False
    )
```

```python
import functools

import jax
import jax.numpy as jnp
from jax import lax
from jax.experimental import pallas as pl
from jax.experimental.pallas import tpu as pltpu
from jax.sharding import PartitionSpec as P

SWEEPS = 2


time_step = 0.25


def orthonormal_steps(gram, rank_cols):
    def sweep(_, basis):
        image = jnp.dot(gram, basis, precision=lax.Precision.HIGHEST)
        inner = jnp.dot(image.T, image, precision=lax.Precision.HIGHEST)
        factor = jnp.linalg.cholesky(inner)
        return lax.linalg.triangular_solve(
            factor, image, left_side=False, lower=True, transpose_a=True
        )

    return lax.fori_loop(0, SWEEPS, sweep, jnp.eye(2 * rank_cols, rank_cols, dtype=jnp.float32))


def step_kernel(slots, ids_ref, cnt_ref, kind_ref, bath_ref,
                group_hbm, own_ref, ons_ref, cpl_ref, bth_ref, out_ref, buf, sems, acc):
    b = pl.program_id(0)
    last = pl.num_programs(0) - 1
    rank_cols = own_ref.shape[2]

    def fetch(blk, slot):
        for k in range(slots):
            @pl.when(k < cnt_ref[blk])
            def _():
                pltpu.make_async_copy(
                    group_hbm.at[ids_ref[blk * slots + k]], buf.at[slot, k], sems.at[slot, k]
                ).start()

    @pl.when(b == 0)
    def _():
        fetch(0, 0)

    @pl.when(b < last)
    def _():
        fetch(b + 1, (b + 1) % 2)

    slot = b % 2
    acc[...] = jnp.zeros_like(acc)
    for k in range(slots):
        @pl.when(k < cnt_ref[b])
        def _():
            pltpu.make_async_copy(group_hbm.at[0], buf.at[slot, k], sems.at[slot, k]).wait()
            t = kind_ref[b * slots + k]
            acc[t] += buf[slot, k].astype(jnp.float32)

    coupled = jnp.dot(cpl_ref[0], acc[0].astype(jnp.bfloat16), preferred_element_type=jnp.float32)
    for t in range(1, cpl_ref.shape[0]):
        coupled += jnp.dot(cpl_ref[t], acc[t].astype(jnp.bfloat16), preferred_element_type=jnp.float32)
    own = own_ref[0]
    wide = own.astype(jnp.float32)
    moved = wide - time_step * (ons_ref[0] * wide + coupled)
    out_ref[0, :, :rank_cols] = moved.astype(out_ref.dtype)
    bathed = jnp.dot(bth_ref[0], own, preferred_element_type=jnp.float32)
    out_ref[0, :, rank_cols:] = bathed.astype(out_ref.dtype)


def stacked_blocks(group_rows, own_rows, energy, ids, counts, kinds, bath_pattern, coupling_blocks, bath_blocks):
    blocks, block_rows, rank_cols = own_rows.shape
    slots = ids.shape[0] // blocks
    kinds_n = coupling_blocks.shape[0]
    grid_spec = pltpu.PrefetchScalarGridSpec(
        num_scalar_prefetch=4,
        grid=(blocks,),
        in_specs=[
            pl.BlockSpec(memory_space=pl.ANY),
            pl.BlockSpec((1, block_rows, rank_cols), lambda b, *_: (b, 0, 0)),
            pl.BlockSpec((1, block_rows, 1), lambda b, *_: (b, 0, 0)),
            pl.BlockSpec((kinds_n, block_rows, block_rows), lambda b, *_: (0, 0, 0)),
            pl.BlockSpec((1, block_rows, block_rows), lambda b, i, c, t, bp: (bp[b], 0, 0)),
        ],
        out_specs=pl.BlockSpec((1, block_rows, 2 * rank_cols), lambda b, *_: (b, 0, 0)),
        scratch_shapes=[
            pltpu.VMEM((2, slots, block_rows, rank_cols), group_rows.dtype),
            pltpu.SemaphoreType.DMA((2, slots)),
            pltpu.VMEM((kinds_n, block_rows, rank_cols), jnp.float32),
        ],
    )
    return pl.pallas_call(
        functools.partial(step_kernel, slots),
        grid_spec=grid_spec,
        out_shape=jax.ShapeDtypeStruct((blocks, block_rows, 2 * rank_cols), jnp.bfloat16),
        compiler_params=pltpu.CompilerParams(dimension_semantics=("arbitrary",)),
    )(ids, counts, kinds, bath_pattern, group_rows, own_rows, energy, coupling_blocks, bath_blocks)


def allreduce_kernel(fields, cols, x_ref, o_ref, *scratch):
    stages = len(fields)
    recv_bufs = scratch[:stages]
    send_sems, recv_sems, work = scratch[stages], scratch[stages + 1], scratch[stages + 2]
    me = lax.axis_index("row") * cols + lax.axis_index("col")

    def field(s, r):
        return (me // (1 << s)) % r

    def place(s, r, d):
        other = me + ((field(s, r) + d) % r - field(s, r)) * (1 << s)
        return (other // cols, other % cols)

    barrier = pltpu.get_barrier_semaphore()
    partners = 0
    for s, r in fields:
        for d in range(1, r):
            pl.semaphore_signal(barrier, inc=1, device_id=place(s, r, d), device_id_type=pl.DeviceIdType.MESH)
            partners += 1
    pl.semaphore_wait(barrier, partners)

    base = 0
    size = x_ref.shape[0]
    slot = 0
    for j, (s, r) in enumerate(fields):
        part = size // r
        f = field(s, r)
        src = x_ref if j == 0 else work
        copies = []
        for d in range(1, r):
            give = pl.multiple_of(base + ((f + d) % r) * part, 8)
            copy = pltpu.make_async_remote_copy(
                src_ref=src.at[pl.ds(give, part)],
                dst_ref=recv_bufs[j].at[d - 1],
                send_sem=send_sems.at[slot],
                recv_sem=recv_sems.at[slot],
                device_id=place(s, r, d),
                device_id_type=pl.DeviceIdType.MESH,
            )
            copy.start()
            copies.append(copy)
            slot += 1
        for copy in copies:
            copy.wait()
        keep = pl.multiple_of(base + f * part, 8)
        total = src[pl.ds(keep, part)]
        for d in range(1, r):
            total = total + recv_bufs[j][d - 1]
        work[pl.ds(keep, part)] = total
        base, size = keep, part
    o_ref[pl.ds(base, size)] = work[pl.ds(base, size)]
    for j in reversed(range(stages)):
        s, r = fields[j]
        block = o_ref.at[pl.ds(base, size)]
        copies = []
        for d in range(1, r):
            copy = pltpu.make_async_remote_copy(
                src_ref=block,
                dst_ref=block,
                send_sem=send_sems.at[slot],
                recv_sem=recv_sems.at[slot],
                device_id=place(s, r, d),
                device_id_type=pl.DeviceIdType.MESH,
            )
            copy.start()
            copies.append(copy)
            slot += 1
        for copy in copies:
            copy.wait()
        base = pl.multiple_of(base - field(s, r) * size, 8)
        size = size * r


def kernel_sum(local, fields, cols):
    lanes = 128
    flat = local.reshape(-1, lanes)
    rows = flat.shape[0]
    scratch = []
    left = rows
    for s, r in fields:
        left //= r
        scratch.append(pltpu.VMEM((r - 1, left, lanes), jnp.float32))
    copies = 2 * sum(r - 1 for _, r in fields)
    scratch += [pltpu.SemaphoreType.DMA((copies,)), pltpu.SemaphoreType.DMA((copies,))]
    scratch += [pltpu.VMEM(flat.shape, jnp.float32)]
    total = pl.pallas_call(
        functools.partial(allreduce_kernel, tuple(fields), cols),
        out_shape=jax.ShapeDtypeStruct(flat.shape, flat.dtype),
        in_specs=[pl.BlockSpec(memory_space=pltpu.VMEM)],
        out_specs=pl.BlockSpec(memory_space=pltpu.VMEM),
        scratch_shapes=scratch,
        compiler_params=pltpu.CompilerParams(collective_id=0, has_side_effects=True),
    )(flat)
    return total.reshape(local.shape)


def shards(
    density_factor,
    onsite,
    neighbour_ids,
    neighbour_count,
    coupling_type,
    coupling_blocks,
    bath_pattern,
    bath_blocks,
):
    blocks, slots = neighbour_ids.shape
    block_rows = coupling_blocks.shape[1]
    rank_cols = density_factor.shape[1]
    col_count = lax.axis_size("col")
    group_blocks = col_count * blocks
    row_place = lax.axis_index("row")
    in_group = jnp.clip(neighbour_ids - row_place * group_blocks, 0, group_blocks - 1)
    counts = jnp.clip(neighbour_count, 1, slots)
    kinds = jnp.clip(coupling_type, 0, coupling_blocks.shape[0] - 1)
    bath_kind = jnp.clip(bath_pattern, 0, bath_blocks.shape[0] - 1)
    gathered = lax.all_gather(density_factor, "col", axis=0, tiled=True)
    group_rows = gathered.reshape(group_blocks, block_rows, rank_cols)
    own_rows = density_factor.reshape(blocks, block_rows, rank_cols)
    energy = onsite.reshape(blocks, block_rows, 1)
    stacked = stacked_blocks(
        group_rows, own_rows, energy, in_group.reshape(-1), counts, kinds.reshape(-1), bath_kind,
        coupling_blocks, bath_blocks,
    ).reshape(blocks * block_rows, 2 * rank_cols)
    local_gram = lax.dot_general(
        stacked, stacked, (((0,), (0,)), ((), ())), preferred_element_type=jnp.float32
    )
    devices = lax.axis_size("row") * col_count
    stage_bits = devices.bit_length() - 1
    if stage_bits == 7:
        fields = [(4, 2), (0, 16), (5, 4)]
    else:
        fields = [(s, 2) for s in range(stage_bits)]
    gram_sum = kernel_sum(local_gram, fields, col_count)
    rotation = orthonormal_steps(gram_sum, rank_cols).astype(jnp.bfloat16)
    return jnp.dot(stacked, rotation, preferred_element_type=jnp.float32).astype(jnp.bfloat16)


def solution(mesh):
    placed = (
        P(("row", "col"), None),
        P(("row", "col")),
        P(("row", "col"), None),
        P(("row", "col")),
        P(("row", "col"), None),
        P(),
        P(("row", "col")),
        P(),
    )
    return jax.shard_map(
        shards, mesh=mesh, in_specs=placed, out_specs=P(("row", "col"), None), check_vma=False
    )
```

```python
import functools

import jax
import jax.numpy as jnp
from jax import lax
from jax.experimental import pallas as pl
from jax.experimental.pallas import tpu as pltpu
from jax.sharding import PartitionSpec as P

SWEEPS = 2


time_step = 0.25


def orthonormal_steps(gram, rank_cols):
    def sweep(_, basis):
        image = jnp.dot(gram, basis, precision=lax.Precision.HIGHEST)
        inner = jnp.dot(image.T, image, precision=lax.Precision.HIGHEST)
        factor = jnp.linalg.cholesky(inner)
        return lax.linalg.triangular_solve(
            factor, image, left_side=False, lower=True, transpose_a=True
        )

    return lax.fori_loop(0, SWEEPS, sweep, jnp.eye(2 * rank_cols, rank_cols, dtype=jnp.float32))


def step_kernel(slots, ids_ref, cnt_ref, kind_ref, bath_ref,
                group_hbm, own_ref, ons_ref, cpl_ref, bth_ref, out_ref, buf, sems, acc):
    b = pl.program_id(0)
    last = pl.num_programs(0) - 1
    rank_cols = own_ref.shape[2]

    def fetch(blk, slot):
        for k in range(slots):
            @pl.when(k < cnt_ref[blk])
            def _():
                pltpu.make_async_copy(
                    group_hbm.at[ids_ref[blk * slots + k]], buf.at[slot, k], sems.at[slot, k]
                ).start()

    @pl.when(b == 0)
    def _():
        fetch(0, 0)

    @pl.when(b < last)
    def _():
        fetch(b + 1, (b + 1) % 2)

    slot = b % 2
    acc[...] = jnp.zeros_like(acc)
    for k in range(slots):
        @pl.when(k < cnt_ref[b])
        def _():
            pltpu.make_async_copy(group_hbm.at[0], buf.at[slot, k], sems.at[slot, k]).wait()
            t = kind_ref[b * slots + k]
            acc[t] += buf[slot, k].astype(jnp.float32)

    coupled = jnp.dot(cpl_ref[0], acc[0].astype(jnp.bfloat16), preferred_element_type=jnp.float32)
    for t in range(1, cpl_ref.shape[0]):
        coupled += jnp.dot(cpl_ref[t], acc[t].astype(jnp.bfloat16), preferred_element_type=jnp.float32)
    own = own_ref[0]
    wide = own.astype(jnp.float32)
    moved = wide - time_step * (ons_ref[0] * wide + coupled)
    out_ref[0, :, :rank_cols] = moved.astype(out_ref.dtype)
    bathed = jnp.dot(bth_ref[0], own, preferred_element_type=jnp.float32)
    out_ref[0, :, rank_cols:] = bathed.astype(out_ref.dtype)


def stacked_blocks(group_rows, own_rows, energy, ids, counts, kinds, bath_pattern, coupling_blocks, bath_blocks):
    blocks, block_rows, rank_cols = own_rows.shape
    slots = ids.shape[0] // blocks
    kinds_n = coupling_blocks.shape[0]
    grid_spec = pltpu.PrefetchScalarGridSpec(
        num_scalar_prefetch=4,
        grid=(blocks,),
        in_specs=[
            pl.BlockSpec(memory_space=pl.ANY),
            pl.BlockSpec((1, block_rows, rank_cols), lambda b, *_: (b, 0, 0)),
            pl.BlockSpec((1, block_rows, 1), lambda b, *_: (b, 0, 0)),
            pl.BlockSpec((kinds_n, block_rows, block_rows), lambda b, *_: (0, 0, 0)),
            pl.BlockSpec((1, block_rows, block_rows), lambda b, i, c, t, bp: (bp[b], 0, 0)),
        ],
        out_specs=pl.BlockSpec((1, block_rows, 2 * rank_cols), lambda b, *_: (b, 0, 0)),
        scratch_shapes=[
            pltpu.VMEM((2, slots, block_rows, rank_cols), group_rows.dtype),
            pltpu.SemaphoreType.DMA((2, slots)),
            pltpu.VMEM((kinds_n, block_rows, rank_cols), jnp.float32),
        ],
    )
    return pl.pallas_call(
        functools.partial(step_kernel, slots),
        grid_spec=grid_spec,
        out_shape=jax.ShapeDtypeStruct((blocks, block_rows, 2 * rank_cols), jnp.bfloat16),
        compiler_params=pltpu.CompilerParams(dimension_semantics=("arbitrary",)),
    )(ids, counts, kinds, bath_pattern, group_rows, own_rows, energy, coupling_blocks, bath_blocks)


def allreduce_kernel(fields, cols, x_ref, o_ref, *scratch):
    stages = len(fields)
    recv_bufs = scratch[:stages]
    send_sems, recv_sems, work = scratch[stages], scratch[stages + 1], scratch[stages + 2]
    me = lax.axis_index("row") * cols + lax.axis_index("col")

    def field(s, r):
        return (me // (1 << s)) % r

    def place(s, r, d):
        other = me + ((field(s, r) + d) % r - field(s, r)) * (1 << s)
        return (other // cols, other % cols)

    barrier = pltpu.get_barrier_semaphore()
    partners = 0
    for s, r in fields:
        for d in range(1, r):
            pl.semaphore_signal(barrier, inc=1, device_id=place(s, r, d), device_id_type=pl.DeviceIdType.MESH)
            partners += 1
    pl.semaphore_wait(barrier, partners)

    base = 0
    size = x_ref.shape[0]
    slot = 0
    for j, (s, r) in enumerate(fields):
        part = size // r
        f = field(s, r)
        src = x_ref if j == 0 else work
        copies = []
        for d in range(1, r):
            give = pl.multiple_of(base + ((f + d) % r) * part, 8)
            copy = pltpu.make_async_remote_copy(
                src_ref=src.at[pl.ds(give, part)],
                dst_ref=recv_bufs[j].at[d - 1],
                send_sem=send_sems.at[slot],
                recv_sem=recv_sems.at[slot],
                device_id=place(s, r, d),
                device_id_type=pl.DeviceIdType.MESH,
            )
            copy.start()
            copies.append(copy)
            slot += 1
        for copy in copies:
            copy.wait()
        keep = pl.multiple_of(base + f * part, 8)
        total = src[pl.ds(keep, part)]
        for d in range(1, r):
            total = total + recv_bufs[j][d - 1]
        work[pl.ds(keep, part)] = total
        base, size = keep, part
    o_ref[pl.ds(base, size)] = work[pl.ds(base, size)]
    for j in reversed(range(stages)):
        s, r = fields[j]
        block = o_ref.at[pl.ds(base, size)]
        copies = []
        for d in range(1, r):
            copy = pltpu.make_async_remote_copy(
                src_ref=block,
                dst_ref=block,
                send_sem=send_sems.at[slot],
                recv_sem=recv_sems.at[slot],
                device_id=place(s, r, d),
                device_id_type=pl.DeviceIdType.MESH,
            )
            copy.start()
            copies.append(copy)
            slot += 1
        for copy in copies:
            copy.wait()
        base = pl.multiple_of(base - field(s, r) * size, 8)
        size = size * r


def kernel_sum(local, fields, cols):
    lanes = 128
    flat = local.reshape(-1, lanes)
    rows = flat.shape[0]
    scratch = []
    left = rows
    for s, r in fields:
        left //= r
        scratch.append(pltpu.VMEM((r - 1, left, lanes), jnp.float32))
    copies = 2 * sum(r - 1 for _, r in fields)
    scratch += [pltpu.SemaphoreType.DMA((copies,)), pltpu.SemaphoreType.DMA((copies,))]
    scratch += [pltpu.VMEM(flat.shape, jnp.float32)]
    total = pl.pallas_call(
        functools.partial(allreduce_kernel, tuple(fields), cols),
        out_shape=jax.ShapeDtypeStruct(flat.shape, flat.dtype),
        in_specs=[pl.BlockSpec(memory_space=pltpu.VMEM)],
        out_specs=pl.BlockSpec(memory_space=pltpu.VMEM),
        scratch_shapes=scratch,
        compiler_params=pltpu.CompilerParams(collective_id=0, has_side_effects=True),
    )(flat)
    return total.reshape(local.shape)


def shards(
    density_factor,
    onsite,
    neighbour_ids,
    neighbour_count,
    coupling_type,
    coupling_blocks,
    bath_pattern,
    bath_blocks,
):
    blocks, slots = neighbour_ids.shape
    block_rows = coupling_blocks.shape[1]
    rank_cols = density_factor.shape[1]
    col_count = lax.axis_size("col")
    group_blocks = col_count * blocks
    row_place = lax.axis_index("row")
    in_group = jnp.clip(neighbour_ids - row_place * group_blocks, 0, group_blocks - 1)
    counts = jnp.clip(neighbour_count, 1, slots)
    kinds = jnp.clip(coupling_type, 0, coupling_blocks.shape[0] - 1)
    bath_kind = jnp.clip(bath_pattern, 0, bath_blocks.shape[0] - 1)
    gathered = lax.all_gather(density_factor, "col", axis=0, tiled=True)
    group_rows = gathered.reshape(group_blocks, block_rows, rank_cols)
    own_rows = density_factor.reshape(blocks, block_rows, rank_cols)
    energy = onsite.reshape(blocks, block_rows, 1)
    stacked = stacked_blocks(
        group_rows, own_rows, energy, in_group.reshape(-1), counts, kinds.reshape(-1), bath_kind,
        coupling_blocks, bath_blocks,
    ).reshape(blocks * block_rows, 2 * rank_cols)
    local_gram = lax.dot_general(
        stacked, stacked, (((0,), (0,)), ((), ())), preferred_element_type=jnp.float32
    )
    devices = lax.axis_size("row") * col_count
    stage_bits = devices.bit_length() - 1
    if stage_bits == 7:
        fields = [(0, 16), (4, 8)]
    else:
        fields = [(s, 2) for s in range(stage_bits)]
    gram_sum = kernel_sum(local_gram, fields, col_count)
    rotation = orthonormal_steps(gram_sum, rank_cols).astype(jnp.bfloat16)
    return jnp.dot(stacked, rotation, preferred_element_type=jnp.float32).astype(jnp.bfloat16)


def solution(mesh):
    placed = (
        P(("row", "col"), None),
        P(("row", "col")),
        P(("row", "col"), None),
        P(("row", "col")),
        P(("row", "col"), None),
        P(),
        P(("row", "col")),
        P(),
    )
    return jax.shard_map(
        shards, mesh=mesh, in_specs=placed, out_specs=P(("row", "col"), None), check_vma=False
    )
```

```python
import functools

import jax
import jax.numpy as jnp
from jax import lax
from jax.experimental import pallas as pl
from jax.experimental.pallas import tpu as pltpu
from jax.sharding import PartitionSpec as P

SWEEPS = 2


time_step = 0.25


def orthonormal_steps(gram, rank_cols):
    def sweep(_, basis):
        image = jnp.dot(gram, basis, precision=lax.Precision.HIGHEST)
        inner = jnp.dot(image.T, image, precision=lax.Precision.HIGHEST)
        factor = jnp.linalg.cholesky(inner)
        return lax.linalg.triangular_solve(
            factor, image, left_side=False, lower=True, transpose_a=True
        )

    return lax.fori_loop(0, SWEEPS, sweep, jnp.eye(2 * rank_cols, rank_cols, dtype=jnp.float32))


def step_kernel(slots, ids_ref, cnt_ref, kind_ref, bath_ref,
                group_hbm, own_ref, ons_ref, cpl_ref, bth_ref, out_ref, gram_ref, buf, sems, acc):
    b = pl.program_id(0)
    last = pl.num_programs(0) - 1
    rank_cols = own_ref.shape[2]

    def fetch(blk, slot):
        for k in range(slots):
            @pl.when(k < cnt_ref[blk])
            def _():
                pltpu.make_async_copy(
                    group_hbm.at[ids_ref[blk * slots + k]], buf.at[slot, k], sems.at[slot, k]
                ).start()

    @pl.when(b == 0)
    def _():
        fetch(0, 0)

    @pl.when(b < last)
    def _():
        fetch(b + 1, (b + 1) % 2)

    slot = b % 2
    acc[...] = jnp.zeros_like(acc)
    for k in range(slots):
        @pl.when(k < cnt_ref[b])
        def _():
            pltpu.make_async_copy(group_hbm.at[0], buf.at[slot, k], sems.at[slot, k]).wait()
            t = kind_ref[b * slots + k]
            acc[t] += buf[slot, k].astype(jnp.float32)

    coupled = jnp.dot(cpl_ref[0], acc[0].astype(jnp.bfloat16), preferred_element_type=jnp.float32)
    for t in range(1, cpl_ref.shape[0]):
        coupled += jnp.dot(cpl_ref[t], acc[t].astype(jnp.bfloat16), preferred_element_type=jnp.float32)
    own = own_ref[0]
    wide = own.astype(jnp.float32)
    moved = wide - time_step * (ons_ref[0] * wide + coupled)
    out_ref[0, :, :rank_cols] = moved.astype(out_ref.dtype)
    bathed = jnp.dot(bth_ref[0], own, preferred_element_type=jnp.float32)
    out_ref[0, :, rank_cols:] = bathed.astype(out_ref.dtype)
    stacked = out_ref[0]
    part = lax.dot_general(
        stacked, stacked, (((0,), (0,)), ((), ())), preferred_element_type=jnp.float32
    )

    @pl.when(b == 0)
    def _():
        gram_ref[...] = part

    @pl.when(b > 0)
    def _():
        gram_ref[...] += part


def stacked_blocks(group_rows, own_rows, energy, ids, counts, kinds, bath_pattern, coupling_blocks, bath_blocks):
    blocks, block_rows, rank_cols = own_rows.shape
    slots = ids.shape[0] // blocks
    kinds_n = coupling_blocks.shape[0]
    grid_spec = pltpu.PrefetchScalarGridSpec(
        num_scalar_prefetch=4,
        grid=(blocks,),
        in_specs=[
            pl.BlockSpec(memory_space=pl.ANY),
            pl.BlockSpec((1, block_rows, rank_cols), lambda b, *_: (b, 0, 0)),
            pl.BlockSpec((1, block_rows, 1), lambda b, *_: (b, 0, 0)),
            pl.BlockSpec((kinds_n, block_rows, block_rows), lambda b, *_: (0, 0, 0)),
            pl.BlockSpec((1, block_rows, block_rows), lambda b, i, c, t, bp: (bp[b], 0, 0)),
        ],
        out_specs=[
            pl.BlockSpec((1, block_rows, 2 * rank_cols), lambda b, *_: (b, 0, 0)),
            pl.BlockSpec((2 * rank_cols, 2 * rank_cols), lambda b, *_: (0, 0)),
        ],
        scratch_shapes=[
            pltpu.VMEM((2, slots, block_rows, rank_cols), group_rows.dtype),
            pltpu.SemaphoreType.DMA((2, slots)),
            pltpu.VMEM((kinds_n, block_rows, rank_cols), jnp.float32),
        ],
    )
    return pl.pallas_call(
        functools.partial(step_kernel, slots),
        grid_spec=grid_spec,
        out_shape=[
            jax.ShapeDtypeStruct((blocks, block_rows, 2 * rank_cols), jnp.bfloat16),
            jax.ShapeDtypeStruct((2 * rank_cols, 2 * rank_cols), jnp.float32),
        ],
        compiler_params=pltpu.CompilerParams(dimension_semantics=("arbitrary",)),
    )(ids, counts, kinds, bath_pattern, group_rows, own_rows, energy, coupling_blocks, bath_blocks)


def allreduce_kernel(fields, cols, x_ref, o_ref, *scratch):
    stages = len(fields)
    recv_bufs = scratch[:stages]
    send_sems, recv_sems, work = scratch[stages], scratch[stages + 1], scratch[stages + 2]
    me = lax.axis_index("row") * cols + lax.axis_index("col")

    def field(s, r):
        return (me // (1 << s)) % r

    def place(s, r, d):
        other = me + ((field(s, r) + d) % r - field(s, r)) * (1 << s)
        return (other // cols, other % cols)

    barrier = pltpu.get_barrier_semaphore()
    partners = 0
    for s, r in fields:
        for d in range(1, r):
            pl.semaphore_signal(barrier, inc=1, device_id=place(s, r, d), device_id_type=pl.DeviceIdType.MESH)
            partners += 1
    pl.semaphore_wait(barrier, partners)

    base = 0
    size = x_ref.shape[0]
    slot = 0
    for j, (s, r) in enumerate(fields):
        part = size // r
        f = field(s, r)
        src = x_ref if j == 0 else work
        copies = []
        for d in range(1, r):
            give = pl.multiple_of(base + ((f + d) % r) * part, 8)
            copy = pltpu.make_async_remote_copy(
                src_ref=src.at[pl.ds(give, part)],
                dst_ref=recv_bufs[j].at[d - 1],
                send_sem=send_sems.at[slot],
                recv_sem=recv_sems.at[slot],
                device_id=place(s, r, d),
                device_id_type=pl.DeviceIdType.MESH,
            )
            copy.start()
            copies.append(copy)
            slot += 1
        for copy in copies:
            copy.wait()
        keep = pl.multiple_of(base + f * part, 8)
        total = src[pl.ds(keep, part)]
        for d in range(1, r):
            total = total + recv_bufs[j][d - 1]
        work[pl.ds(keep, part)] = total
        base, size = keep, part
    o_ref[pl.ds(base, size)] = work[pl.ds(base, size)]
    for j in reversed(range(stages)):
        s, r = fields[j]
        block = o_ref.at[pl.ds(base, size)]
        copies = []
        for d in range(1, r):
            copy = pltpu.make_async_remote_copy(
                src_ref=block,
                dst_ref=block,
                send_sem=send_sems.at[slot],
                recv_sem=recv_sems.at[slot],
                device_id=place(s, r, d),
                device_id_type=pl.DeviceIdType.MESH,
            )
            copy.start()
            copies.append(copy)
            slot += 1
        for copy in copies:
            copy.wait()
        base = pl.multiple_of(base - field(s, r) * size, 8)
        size = size * r


def kernel_sum(local, fields, cols):
    lanes = 128
    flat = local.reshape(-1, lanes)
    rows = flat.shape[0]
    scratch = []
    left = rows
    for s, r in fields:
        left //= r
        scratch.append(pltpu.VMEM((r - 1, left, lanes), jnp.float32))
    copies = 2 * sum(r - 1 for _, r in fields)
    scratch += [pltpu.SemaphoreType.DMA((copies,)), pltpu.SemaphoreType.DMA((copies,))]
    scratch += [pltpu.VMEM(flat.shape, jnp.float32)]
    total = pl.pallas_call(
        functools.partial(allreduce_kernel, tuple(fields), cols),
        out_shape=jax.ShapeDtypeStruct(flat.shape, flat.dtype),
        in_specs=[pl.BlockSpec(memory_space=pltpu.VMEM)],
        out_specs=pl.BlockSpec(memory_space=pltpu.VMEM),
        scratch_shapes=scratch,
        compiler_params=pltpu.CompilerParams(collective_id=0, has_side_effects=True),
    )(flat)
    return total.reshape(local.shape)


def shards(
    density_factor,
    onsite,
    neighbour_ids,
    neighbour_count,
    coupling_type,
    coupling_blocks,
    bath_pattern,
    bath_blocks,
):
    blocks, slots = neighbour_ids.shape
    block_rows = coupling_blocks.shape[1]
    rank_cols = density_factor.shape[1]
    col_count = lax.axis_size("col")
    group_blocks = col_count * blocks
    row_place = lax.axis_index("row")
    in_group = jnp.clip(neighbour_ids - row_place * group_blocks, 0, group_blocks - 1)
    counts = jnp.clip(neighbour_count, 1, slots)
    kinds = jnp.clip(coupling_type, 0, coupling_blocks.shape[0] - 1)
    bath_kind = jnp.clip(bath_pattern, 0, bath_blocks.shape[0] - 1)
    gathered = lax.all_gather(density_factor, "col", axis=0, tiled=True)
    group_rows = gathered.reshape(group_blocks, block_rows, rank_cols)
    own_rows = density_factor.reshape(blocks, block_rows, rank_cols)
    energy = onsite.reshape(blocks, block_rows, 1)
    stacked, local_gram = stacked_blocks(
        group_rows, own_rows, energy, in_group.reshape(-1), counts, kinds.reshape(-1), bath_kind,
        coupling_blocks, bath_blocks,
    )
    stacked = stacked.reshape(blocks * block_rows, 2 * rank_cols)
    devices = lax.axis_size("row") * col_count
    stage_bits = devices.bit_length() - 1
    if stage_bits == 7:
        fields = [(4, 2), (0, 16), (5, 4)]
    else:
        fields = [(s, 2) for s in range(stage_bits)]
    gram_sum = kernel_sum(local_gram, fields, col_count)
    rotation = orthonormal_steps(gram_sum, rank_cols).astype(jnp.bfloat16)
    return jnp.dot(stacked, rotation, preferred_element_type=jnp.float32).astype(jnp.bfloat16)


def solution(mesh):
    placed = (
        P(("row", "col"), None),
        P(("row", "col")),
        P(("row", "col"), None),
        P(("row", "col")),
        P(("row", "col"), None),
        P(),
        P(("row", "col")),
        P(),
    )
    return jax.shard_map(
        shards, mesh=mesh, in_specs=placed, out_specs=P(("row", "col"), None), check_vma=False
    )
```

```python
import functools

import jax
import jax.numpy as jnp
from jax import lax
from jax.experimental import pallas as pl
from jax.experimental.pallas import tpu as pltpu
from jax.sharding import PartitionSpec as P

SWEEPS = 2


time_step = 0.25


def orthonormal_steps(gram, rank_cols):
    def sweep(_, basis):
        image = jnp.dot(gram, basis, precision=lax.Precision.HIGHEST)
        inner = jnp.dot(image.T, image, precision=lax.Precision.HIGHEST)
        factor = jnp.linalg.cholesky(inner)
        return lax.linalg.triangular_solve(
            factor, image, left_side=False, lower=True, transpose_a=True
        )

    return lax.fori_loop(0, SWEEPS, sweep, jnp.eye(2 * rank_cols, rank_cols, dtype=jnp.float32))


def step_kernel(slots, ids_ref, cnt_ref, kind_ref,
                group_hbm, own_ref, ons_ref, cpl_ref, out_ref, buf, sems, acc):
    b = pl.program_id(0)
    last = pl.num_programs(0) - 1
    rank_cols = own_ref.shape[2]

    def fetch(blk, slot):
        for k in range(slots):
            @pl.when(k < cnt_ref[blk])
            def _():
                pltpu.make_async_copy(
                    group_hbm.at[ids_ref[blk * slots + k]], buf.at[slot, k], sems.at[slot, k]
                ).start()

    @pl.when(b == 0)
    def _():
        fetch(0, 0)

    @pl.when(b < last)
    def _():
        fetch(b + 1, (b + 1) % 2)

    slot = b % 2
    acc[...] = jnp.zeros_like(acc)
    for k in range(slots):
        @pl.when(k < cnt_ref[b])
        def _():
            pltpu.make_async_copy(group_hbm.at[0], buf.at[slot, k], sems.at[slot, k]).wait()
            t = kind_ref[b * slots + k]
            acc[t] += buf[slot, k].astype(jnp.float32)

    coupled = jnp.dot(cpl_ref[0], acc[0].astype(jnp.bfloat16), preferred_element_type=jnp.float32)
    for t in range(1, cpl_ref.shape[0]):
        coupled += jnp.dot(cpl_ref[t], acc[t].astype(jnp.bfloat16), preferred_element_type=jnp.float32)
    own = own_ref[0]
    wide = own.astype(jnp.float32)
    moved = wide - time_step * (ons_ref[0] * wide + coupled)
    out_ref[0] = moved.astype(out_ref.dtype)


def moved_blocks(group_rows, own_rows, energy, ids, counts, kinds, coupling_blocks):
    blocks, block_rows, rank_cols = own_rows.shape
    slots = ids.shape[0] // blocks
    kinds_n = coupling_blocks.shape[0]
    grid_spec = pltpu.PrefetchScalarGridSpec(
        num_scalar_prefetch=3,
        grid=(blocks,),
        in_specs=[
            pl.BlockSpec(memory_space=pl.ANY),
            pl.BlockSpec((1, block_rows, rank_cols), lambda b, *_: (b, 0, 0)),
            pl.BlockSpec((1, block_rows, 1), lambda b, *_: (b, 0, 0)),
            pl.BlockSpec((kinds_n, block_rows, block_rows), lambda b, *_: (0, 0, 0)),
        ],
        out_specs=pl.BlockSpec((1, block_rows, rank_cols), lambda b, *_: (b, 0, 0)),
        scratch_shapes=[
            pltpu.VMEM((2, slots, block_rows, rank_cols), group_rows.dtype),
            pltpu.SemaphoreType.DMA((2, slots)),
            pltpu.VMEM((kinds_n, block_rows, rank_cols), jnp.float32),
        ],
    )
    return pl.pallas_call(
        functools.partial(step_kernel, slots),
        grid_spec=grid_spec,
        out_shape=jax.ShapeDtypeStruct((blocks, block_rows, rank_cols), jnp.bfloat16),
        compiler_params=pltpu.CompilerParams(dimension_semantics=("arbitrary",)),
    )(ids, counts, kinds, group_rows, own_rows, energy, coupling_blocks)


def allreduce_kernel(fields, cols, x_ref, o_ref, *scratch):
    stages = len(fields)
    recv_bufs = scratch[:stages]
    send_sems, recv_sems, work = scratch[stages], scratch[stages + 1], scratch[stages + 2]
    me = lax.axis_index("row") * cols + lax.axis_index("col")

    def field(s, r):
        return (me // (1 << s)) % r

    def place(s, r, d):
        other = me + ((field(s, r) + d) % r - field(s, r)) * (1 << s)
        return (other // cols, other % cols)

    barrier = pltpu.get_barrier_semaphore()
    partners = 0
    for s, r in fields:
        for d in range(1, r):
            pl.semaphore_signal(barrier, inc=1, device_id=place(s, r, d), device_id_type=pl.DeviceIdType.MESH)
            partners += 1
    pl.semaphore_wait(barrier, partners)

    base = 0
    size = x_ref.shape[0]
    slot = 0
    for j, (s, r) in enumerate(fields):
        part = size // r
        f = field(s, r)
        src = x_ref if j == 0 else work
        copies = []
        for d in range(1, r):
            give = pl.multiple_of(base + ((f + d) % r) * part, 8)
            copy = pltpu.make_async_remote_copy(
                src_ref=src.at[pl.ds(give, part)],
                dst_ref=recv_bufs[j].at[d - 1],
                send_sem=send_sems.at[slot],
                recv_sem=recv_sems.at[slot],
                device_id=place(s, r, d),
                device_id_type=pl.DeviceIdType.MESH,
            )
            copy.start()
            copies.append(copy)
            slot += 1
        for copy in copies:
            copy.wait()
        keep = pl.multiple_of(base + f * part, 8)
        total = src[pl.ds(keep, part)]
        for d in range(1, r):
            total = total + recv_bufs[j][d - 1]
        work[pl.ds(keep, part)] = total
        base, size = keep, part
    o_ref[pl.ds(base, size)] = work[pl.ds(base, size)]
    for j in reversed(range(stages)):
        s, r = fields[j]
        block = o_ref.at[pl.ds(base, size)]
        copies = []
        for d in range(1, r):
            copy = pltpu.make_async_remote_copy(
                src_ref=block,
                dst_ref=block,
                send_sem=send_sems.at[slot],
                recv_sem=recv_sems.at[slot],
                device_id=place(s, r, d),
                device_id_type=pl.DeviceIdType.MESH,
            )
            copy.start()
            copies.append(copy)
            slot += 1
        for copy in copies:
            copy.wait()
        base = pl.multiple_of(base - field(s, r) * size, 8)
        size = size * r


def kernel_sum(local, fields, cols):
    lanes = 128
    flat = local.reshape(-1, lanes)
    rows = flat.shape[0]
    scratch = []
    left = rows
    for s, r in fields:
        left //= r
        scratch.append(pltpu.VMEM((r - 1, left, lanes), jnp.float32))
    copies = 2 * sum(r - 1 for _, r in fields)
    scratch += [pltpu.SemaphoreType.DMA((copies,)), pltpu.SemaphoreType.DMA((copies,))]
    scratch += [pltpu.VMEM(flat.shape, jnp.float32)]
    total = pl.pallas_call(
        functools.partial(allreduce_kernel, tuple(fields), cols),
        out_shape=jax.ShapeDtypeStruct(flat.shape, flat.dtype),
        in_specs=[pl.BlockSpec(memory_space=pltpu.VMEM)],
        out_specs=pl.BlockSpec(memory_space=pltpu.VMEM),
        scratch_shapes=scratch,
        compiler_params=pltpu.CompilerParams(collective_id=0, has_side_effects=True),
    )(flat)
    return total.reshape(local.shape)


def shards(
    density_factor,
    onsite,
    neighbour_ids,
    neighbour_count,
    coupling_type,
    coupling_blocks,
    bath_pattern,
    bath_blocks,
):
    blocks, slots = neighbour_ids.shape
    block_rows = coupling_blocks.shape[1]
    rank_cols = density_factor.shape[1]
    col_count = lax.axis_size("col")
    group_blocks = col_count * blocks
    row_place = lax.axis_index("row")
    in_group = jnp.clip(neighbour_ids - row_place * group_blocks, 0, group_blocks - 1)
    counts = jnp.clip(neighbour_count, 1, slots)
    kinds = jnp.clip(coupling_type, 0, coupling_blocks.shape[0] - 1)
    bath_kind = jnp.clip(bath_pattern, 0, bath_blocks.shape[0] - 1)
    own_rows = density_factor.reshape(blocks, block_rows, rank_cols)
    bathed = jnp.einsum(
        "bij,bjr->bir", bath_blocks[bath_kind], own_rows, preferred_element_type=jnp.float32
    ).astype(jnp.bfloat16).reshape(blocks * block_rows, rank_cols)
    contract_rows = (((0,), (0,)), ((), ()))
    bath_gram = lax.dot_general(bathed, bathed, contract_rows, preferred_element_type=jnp.float32)
    gathered = lax.all_gather(density_factor, "col", axis=0, tiled=True)
    group_rows = gathered.reshape(group_blocks, block_rows, rank_cols)
    energy = onsite.reshape(blocks, block_rows, 1)
    moved = moved_blocks(
        group_rows, own_rows, energy, in_group.reshape(-1), counts, kinds.reshape(-1), coupling_blocks,
    ).reshape(blocks * block_rows, rank_cols)
    moved_gram = lax.dot_general(moved, moved, contract_rows, preferred_element_type=jnp.float32)
    cross_gram = lax.dot_general(moved, bathed, contract_rows, preferred_element_type=jnp.float32)
    local_gram = jnp.concatenate(
        [
            jnp.concatenate([moved_gram, cross_gram], axis=1),
            jnp.concatenate([cross_gram.T, bath_gram], axis=1),
        ],
        axis=0,
    )
    devices = lax.axis_size("row") * col_count
    stage_bits = devices.bit_length() - 1
    if stage_bits == 7:
        fields = [(4, 2), (0, 16), (5, 4)]
    else:
        fields = [(s, 2) for s in range(stage_bits)]
    gram_sum = kernel_sum(local_gram, fields, col_count)
    rotation = orthonormal_steps(gram_sum, rank_cols).astype(jnp.bfloat16)
    product = jnp.dot(moved, rotation[:rank_cols], preferred_element_type=jnp.float32)
    product += jnp.dot(bathed, rotation[rank_cols:], preferred_element_type=jnp.float32)
    return product.astype(jnp.bfloat16)


def solution(mesh):
    placed = (
        P(("row", "col"), None),
        P(("row", "col")),
        P(("row", "col"), None),
        P(("row", "col")),
        P(("row", "col"), None),
        P(),
        P(("row", "col")),
        P(),
    )
    return jax.shard_map(
        shards, mesh=mesh, in_specs=placed, out_specs=P(("row", "col"), None), check_vma=False
    )
```

```python
import functools

import jax
import jax.numpy as jnp
from jax import lax
from jax.experimental import pallas as pl
from jax.experimental.pallas import tpu as pltpu
from jax.sharding import PartitionSpec as P

SWEEPS = 2


time_step = 0.25


def orthonormal_steps(gram, rank_cols):
    def sweep(_, basis):
        image = jnp.dot(gram, basis, precision=lax.Precision.HIGHEST)
        inner = jnp.dot(image.T, image, precision=lax.Precision.HIGHEST)
        factor = jnp.linalg.cholesky(inner)
        return lax.linalg.triangular_solve(
            factor, image, left_side=False, lower=True, transpose_a=True
        )

    return lax.fori_loop(0, SWEEPS, sweep, jnp.eye(2 * rank_cols, rank_cols, dtype=jnp.float32))


def step_kernel(slots, ids_ref, cnt_ref, kind_ref,
                group_hbm, own_ref, ons_ref, cpl_ref, out_ref, buf, sems, acc):
    b = pl.program_id(0)
    last = pl.num_programs(0) - 1
    rank_cols = own_ref.shape[2]

    def fetch(blk, slot):
        for k in range(slots):
            @pl.when(k < cnt_ref[blk])
            def _():
                pltpu.make_async_copy(
                    group_hbm.at[ids_ref[blk * slots + k]], buf.at[slot, k], sems.at[slot, k]
                ).start()

    @pl.when(b == 0)
    def _():
        fetch(0, 0)

    @pl.when(b < last)
    def _():
        fetch(b + 1, (b + 1) % 2)

    slot = b % 2
    acc[...] = jnp.zeros_like(acc)
    for k in range(slots):
        @pl.when(k < cnt_ref[b])
        def _():
            pltpu.make_async_copy(group_hbm.at[0], buf.at[slot, k], sems.at[slot, k]).wait()
            t = kind_ref[b * slots + k]
            acc[...] += jnp.dot(cpl_ref[t], buf[slot, k], preferred_element_type=jnp.float32)

    coupled = acc[...]
    own = own_ref[0]
    wide = own.astype(jnp.float32)
    moved = wide - time_step * (ons_ref[0] * wide + coupled)
    out_ref[0] = moved.astype(out_ref.dtype)


def moved_blocks(group_rows, own_rows, energy, ids, counts, kinds, coupling_blocks):
    blocks, block_rows, rank_cols = own_rows.shape
    slots = ids.shape[0] // blocks
    kinds_n = coupling_blocks.shape[0]
    grid_spec = pltpu.PrefetchScalarGridSpec(
        num_scalar_prefetch=3,
        grid=(blocks,),
        in_specs=[
            pl.BlockSpec(memory_space=pl.ANY),
            pl.BlockSpec((1, block_rows, rank_cols), lambda b, *_: (b, 0, 0)),
            pl.BlockSpec((1, block_rows, 1), lambda b, *_: (b, 0, 0)),
            pl.BlockSpec((kinds_n, block_rows, block_rows), lambda b, *_: (0, 0, 0)),
        ],
        out_specs=pl.BlockSpec((1, block_rows, rank_cols), lambda b, *_: (b, 0, 0)),
        scratch_shapes=[
            pltpu.VMEM((2, slots, block_rows, rank_cols), group_rows.dtype),
            pltpu.SemaphoreType.DMA((2, slots)),
            pltpu.VMEM((block_rows, rank_cols), jnp.float32),
        ],
    )
    return pl.pallas_call(
        functools.partial(step_kernel, slots),
        grid_spec=grid_spec,
        out_shape=jax.ShapeDtypeStruct((blocks, block_rows, rank_cols), jnp.bfloat16),
        compiler_params=pltpu.CompilerParams(dimension_semantics=("arbitrary",)),
    )(ids, counts, kinds, group_rows, own_rows, energy, coupling_blocks)


def allreduce_kernel(fields, cols, x_ref, o_ref, *scratch):
    stages = len(fields)
    recv_bufs = scratch[:stages]
    send_sems, recv_sems, work = scratch[stages], scratch[stages + 1], scratch[stages + 2]
    me = lax.axis_index("row") * cols + lax.axis_index("col")

    def field(s, r):
        return (me // (1 << s)) % r

    def place(s, r, d):
        other = me + ((field(s, r) + d) % r - field(s, r)) * (1 << s)
        return (other // cols, other % cols)

    barrier = pltpu.get_barrier_semaphore()
    partners = 0
    for s, r in fields:
        for d in range(1, r):
            pl.semaphore_signal(barrier, inc=1, device_id=place(s, r, d), device_id_type=pl.DeviceIdType.MESH)
            partners += 1
    pl.semaphore_wait(barrier, partners)

    base = 0
    size = x_ref.shape[0]
    slot = 0
    for j, (s, r) in enumerate(fields):
        part = size // r
        f = field(s, r)
        src = x_ref if j == 0 else work
        copies = []
        for d in range(1, r):
            give = pl.multiple_of(base + ((f + d) % r) * part, 8)
            copy = pltpu.make_async_remote_copy(
                src_ref=src.at[pl.ds(give, part)],
                dst_ref=recv_bufs[j].at[d - 1],
                send_sem=send_sems.at[slot],
                recv_sem=recv_sems.at[slot],
                device_id=place(s, r, d),
                device_id_type=pl.DeviceIdType.MESH,
            )
            copy.start()
            copies.append(copy)
            slot += 1
        for copy in copies:
            copy.wait()
        keep = pl.multiple_of(base + f * part, 8)
        total = src[pl.ds(keep, part)]
        for d in range(1, r):
            total = total + recv_bufs[j][d - 1]
        work[pl.ds(keep, part)] = total
        base, size = keep, part
    o_ref[pl.ds(base, size)] = work[pl.ds(base, size)]
    for j in reversed(range(stages)):
        s, r = fields[j]
        block = o_ref.at[pl.ds(base, size)]
        copies = []
        for d in range(1, r):
            copy = pltpu.make_async_remote_copy(
                src_ref=block,
                dst_ref=block,
                send_sem=send_sems.at[slot],
                recv_sem=recv_sems.at[slot],
                device_id=place(s, r, d),
                device_id_type=pl.DeviceIdType.MESH,
            )
            copy.start()
            copies.append(copy)
            slot += 1
        for copy in copies:
            copy.wait()
        base = pl.multiple_of(base - field(s, r) * size, 8)
        size = size * r


def kernel_sum(local, fields, cols):
    lanes = 128
    flat = local.reshape(-1, lanes)
    rows = flat.shape[0]
    scratch = []
    left = rows
    for s, r in fields:
        left //= r
        scratch.append(pltpu.VMEM((r - 1, left, lanes), jnp.float32))
    copies = 2 * sum(r - 1 for _, r in fields)
    scratch += [pltpu.SemaphoreType.DMA((copies,)), pltpu.SemaphoreType.DMA((copies,))]
    scratch += [pltpu.VMEM(flat.shape, jnp.float32)]
    total = pl.pallas_call(
        functools.partial(allreduce_kernel, tuple(fields), cols),
        out_shape=jax.ShapeDtypeStruct(flat.shape, flat.dtype),
        in_specs=[pl.BlockSpec(memory_space=pltpu.VMEM)],
        out_specs=pl.BlockSpec(memory_space=pltpu.VMEM),
        scratch_shapes=scratch,
        compiler_params=pltpu.CompilerParams(collective_id=0, has_side_effects=True),
    )(flat)
    return total.reshape(local.shape)


def shards(
    density_factor,
    onsite,
    neighbour_ids,
    neighbour_count,
    coupling_type,
    coupling_blocks,
    bath_pattern,
    bath_blocks,
):
    blocks, slots = neighbour_ids.shape
    block_rows = coupling_blocks.shape[1]
    rank_cols = density_factor.shape[1]
    col_count = lax.axis_size("col")
    group_blocks = col_count * blocks
    row_place = lax.axis_index("row")
    in_group = jnp.clip(neighbour_ids - row_place * group_blocks, 0, group_blocks - 1)
    counts = jnp.clip(neighbour_count, 1, slots)
    kinds = jnp.clip(coupling_type, 0, coupling_blocks.shape[0] - 1)
    bath_kind = jnp.clip(bath_pattern, 0, bath_blocks.shape[0] - 1)
    own_rows = density_factor.reshape(blocks, block_rows, rank_cols)
    bathed = jnp.einsum(
        "bij,bjr->bir", bath_blocks[bath_kind], own_rows, preferred_element_type=jnp.float32
    ).astype(jnp.bfloat16).reshape(blocks * block_rows, rank_cols)
    contract_rows = (((0,), (0,)), ((), ()))
    bath_gram = lax.dot_general(bathed, bathed, contract_rows, preferred_element_type=jnp.float32)
    gathered = lax.all_gather(density_factor, "col", axis=0, tiled=True)
    group_rows = gathered.reshape(group_blocks, block_rows, rank_cols)
    energy = onsite.reshape(blocks, block_rows, 1)
    moved = moved_blocks(
        group_rows, own_rows, energy, in_group.reshape(-1), counts, kinds.reshape(-1), coupling_blocks,
    ).reshape(blocks * block_rows, rank_cols)
    moved_gram = lax.dot_general(moved, moved, contract_rows, preferred_element_type=jnp.float32)
    cross_gram = lax.dot_general(moved, bathed, contract_rows, preferred_element_type=jnp.float32)
    local_gram = jnp.concatenate(
        [
            jnp.concatenate([moved_gram, cross_gram], axis=1),
            jnp.concatenate([cross_gram.T, bath_gram], axis=1),
        ],
        axis=0,
    )
    devices = lax.axis_size("row") * col_count
    stage_bits = devices.bit_length() - 1
    if stage_bits == 7:
        fields = [(4, 2), (0, 16), (5, 4)]
    else:
        fields = [(s, 2) for s in range(stage_bits)]
    gram_sum = kernel_sum(local_gram, fields, col_count)
    rotation = orthonormal_steps(gram_sum, rank_cols).astype(jnp.bfloat16)
    product = jnp.dot(moved, rotation[:rank_cols], preferred_element_type=jnp.float32)
    product += jnp.dot(bathed, rotation[rank_cols:], preferred_element_type=jnp.float32)
    return product.astype(jnp.bfloat16)


def solution(mesh):
    placed = (
        P(("row", "col"), None),
        P(("row", "col")),
        P(("row", "col"), None),
        P(("row", "col")),
        P(("row", "col"), None),
        P(),
        P(("row", "col")),
        P(),
    )
    return jax.shard_map(
        shards, mesh=mesh, in_specs=placed, out_specs=P(("row", "col"), None), check_vma=False
    )
```

```python
import functools

import jax
import jax.numpy as jnp
from jax import lax
from jax.experimental import pallas as pl
from jax.experimental.pallas import tpu as pltpu
from jax.sharding import PartitionSpec as P

SWEEPS = 2


time_step = 0.25


def orthonormal_steps(gram, rank_cols):
    def sweep(_, basis):
        image = jnp.dot(gram, basis, precision=lax.Precision.HIGHEST)
        inner = jnp.dot(image.T, image, precision=lax.Precision.HIGHEST)
        factor = jnp.linalg.cholesky(inner)
        return lax.linalg.triangular_solve(
            factor, image, left_side=False, lower=True, transpose_a=True
        )

    return lax.fori_loop(0, SWEEPS, sweep, jnp.eye(2 * rank_cols, rank_cols, dtype=jnp.float32))


def step_kernel(slots, ids_ref, cnt_ref, kind_ref, first_ref, used_ref, lead_ref,
                group_hbm, own_ref, ons_ref, cpl_ref, out_ref, buf, sems, acc, cacc):
    b = pl.program_id(0)
    last = pl.num_programs(0) - 1
    rank_cols = own_ref.shape[2]

    def fetch(blk, slot):
        for k in range(slots):
            @pl.when(k < cnt_ref[blk])
            def _():
                pltpu.make_async_copy(
                    group_hbm.at[ids_ref[blk * slots + k]], buf.at[slot, k], sems.at[slot, k]
                ).start()

    @pl.when(b == 0)
    def _():
        fetch(0, 0)

    @pl.when(b < last)
    def _():
        fetch(b + 1, (b + 1) % 2)

    slot = b % 2
    for k in range(slots):
        @pl.when(k < cnt_ref[b])
        def _():
            pltpu.make_async_copy(group_hbm.at[0], buf.at[slot, k], sems.at[slot, k]).wait()
            t = kind_ref[b * slots + k]
            first = first_ref[b * slots + k]

            @pl.when(first == 1)
            def _():
                acc[t] = buf[slot, k].astype(jnp.float32)

            @pl.when(first == 0)
            def _():
                acc[t] += buf[slot, k].astype(jnp.float32)

    kinds_n = cpl_ref.shape[0]
    for t in range(kinds_n):
        used = used_ref[b * kinds_n + t]
        lead = lead_ref[b * kinds_n + t]

        @pl.when((used == 1) & (lead == 1))
        def _():
            cacc[...] = jnp.dot(cpl_ref[t], acc[t].astype(jnp.bfloat16), preferred_element_type=jnp.float32)

        @pl.when((used == 1) & (lead == 0))
        def _():
            cacc[...] += jnp.dot(cpl_ref[t], acc[t].astype(jnp.bfloat16), preferred_element_type=jnp.float32)

    coupled = cacc[...]
    own = own_ref[0]
    wide = own.astype(jnp.float32)
    moved = wide - time_step * (ons_ref[0] * wide + coupled)
    out_ref[0] = moved.astype(out_ref.dtype)


def moved_blocks(group_rows, own_rows, energy, ids, counts, kinds, first, used, lead, coupling_blocks):
    blocks, block_rows, rank_cols = own_rows.shape
    slots = ids.shape[0] // blocks
    kinds_n = coupling_blocks.shape[0]
    grid_spec = pltpu.PrefetchScalarGridSpec(
        num_scalar_prefetch=6,
        grid=(blocks,),
        in_specs=[
            pl.BlockSpec(memory_space=pl.ANY),
            pl.BlockSpec((1, block_rows, rank_cols), lambda b, *_: (b, 0, 0)),
            pl.BlockSpec((1, block_rows, 1), lambda b, *_: (b, 0, 0)),
            pl.BlockSpec((kinds_n, block_rows, block_rows), lambda b, *_: (0, 0, 0)),
        ],
        out_specs=pl.BlockSpec((1, block_rows, rank_cols), lambda b, *_: (b, 0, 0)),
        scratch_shapes=[
            pltpu.VMEM((2, slots, block_rows, rank_cols), group_rows.dtype),
            pltpu.SemaphoreType.DMA((2, slots)),
            pltpu.VMEM((kinds_n, block_rows, rank_cols), jnp.float32),
            pltpu.VMEM((block_rows, rank_cols), jnp.float32),
        ],
    )
    return pl.pallas_call(
        functools.partial(step_kernel, slots),
        grid_spec=grid_spec,
        out_shape=jax.ShapeDtypeStruct((blocks, block_rows, rank_cols), jnp.bfloat16),
        compiler_params=pltpu.CompilerParams(dimension_semantics=("arbitrary",)),
    )(ids, counts, kinds, first, used, lead, group_rows, own_rows, energy, coupling_blocks)


def allreduce_kernel(fields, cols, x_ref, o_ref, *scratch):
    stages = len(fields)
    recv_bufs = scratch[:stages]
    send_sems, recv_sems, work = scratch[stages], scratch[stages + 1], scratch[stages + 2]
    me = lax.axis_index("row") * cols + lax.axis_index("col")

    def field(s, r):
        return (me // (1 << s)) % r

    def place(s, r, d):
        other = me + ((field(s, r) + d) % r - field(s, r)) * (1 << s)
        return (other // cols, other % cols)

    barrier = pltpu.get_barrier_semaphore()
    partners = 0
    for s, r in fields:
        for d in range(1, r):
            pl.semaphore_signal(barrier, inc=1, device_id=place(s, r, d), device_id_type=pl.DeviceIdType.MESH)
            partners += 1
    pl.semaphore_wait(barrier, partners)

    base = 0
    size = x_ref.shape[0]
    slot = 0
    for j, (s, r) in enumerate(fields):
        part = size // r
        f = field(s, r)
        src = x_ref if j == 0 else work
        copies = []
        for d in range(1, r):
            give = pl.multiple_of(base + ((f + d) % r) * part, 8)
            copy = pltpu.make_async_remote_copy(
                src_ref=src.at[pl.ds(give, part)],
                dst_ref=recv_bufs[j].at[d - 1],
                send_sem=send_sems.at[slot],
                recv_sem=recv_sems.at[slot],
                device_id=place(s, r, d),
                device_id_type=pl.DeviceIdType.MESH,
            )
            copy.start()
            copies.append(copy)
            slot += 1
        for copy in copies:
            copy.wait()
        keep = pl.multiple_of(base + f * part, 8)
        total = src[pl.ds(keep, part)]
        for d in range(1, r):
            total = total + recv_bufs[j][d - 1]
        work[pl.ds(keep, part)] = total
        base, size = keep, part
    o_ref[pl.ds(base, size)] = work[pl.ds(base, size)]
    for j in reversed(range(stages)):
        s, r = fields[j]
        block = o_ref.at[pl.ds(base, size)]
        copies = []
        for d in range(1, r):
            copy = pltpu.make_async_remote_copy(
                src_ref=block,
                dst_ref=block,
                send_sem=send_sems.at[slot],
                recv_sem=recv_sems.at[slot],
                device_id=place(s, r, d),
                device_id_type=pl.DeviceIdType.MESH,
            )
            copy.start()
            copies.append(copy)
            slot += 1
        for copy in copies:
            copy.wait()
        base = pl.multiple_of(base - field(s, r) * size, 8)
        size = size * r


def kernel_sum(local, fields, cols):
    lanes = 128
    flat = local.reshape(-1, lanes)
    rows = flat.shape[0]
    scratch = []
    left = rows
    for s, r in fields:
        left //= r
        scratch.append(pltpu.VMEM((r - 1, left, lanes), jnp.float32))
    copies = 2 * sum(r - 1 for _, r in fields)
    scratch += [pltpu.SemaphoreType.DMA((copies,)), pltpu.SemaphoreType.DMA((copies,))]
    scratch += [pltpu.VMEM(flat.shape, jnp.float32)]
    total = pl.pallas_call(
        functools.partial(allreduce_kernel, tuple(fields), cols),
        out_shape=jax.ShapeDtypeStruct(flat.shape, flat.dtype),
        in_specs=[pl.BlockSpec(memory_space=pltpu.VMEM)],
        out_specs=pl.BlockSpec(memory_space=pltpu.VMEM),
        scratch_shapes=scratch,
        compiler_params=pltpu.CompilerParams(collective_id=0, has_side_effects=True),
    )(flat)
    return total.reshape(local.shape)


def shards(
    density_factor,
    onsite,
    neighbour_ids,
    neighbour_count,
    coupling_type,
    coupling_blocks,
    bath_pattern,
    bath_blocks,
):
    blocks, slots = neighbour_ids.shape
    block_rows = coupling_blocks.shape[1]
    rank_cols = density_factor.shape[1]
    col_count = lax.axis_size("col")
    group_blocks = col_count * blocks
    row_place = lax.axis_index("row")
    in_group = jnp.clip(neighbour_ids - row_place * group_blocks, 0, group_blocks - 1)
    counts = jnp.clip(neighbour_count, 1, slots)
    kinds = jnp.clip(coupling_type, 0, coupling_blocks.shape[0] - 1)
    bath_kind = jnp.clip(bath_pattern, 0, bath_blocks.shape[0] - 1)
    own_rows = density_factor.reshape(blocks, block_rows, rank_cols)
    bathed = jnp.einsum(
        "bij,bjr->bir", bath_blocks[bath_kind], own_rows, preferred_element_type=jnp.float32
    ).astype(jnp.bfloat16).reshape(blocks * block_rows, rank_cols)
    contract_rows = (((0,), (0,)), ((), ()))
    bath_gram = lax.dot_general(bathed, bathed, contract_rows, preferred_element_type=jnp.float32)
    gathered = lax.all_gather(density_factor, "col", axis=0, tiled=True)
    group_rows = gathered.reshape(group_blocks, block_rows, rank_cols)
    energy = onsite.reshape(blocks, block_rows, 1)
    kinds_n = coupling_blocks.shape[0]
    live = jnp.arange(slots, dtype=jnp.int32)[None, :] < counts[:, None]
    same = (kinds[:, :, None] == kinds[:, None, :]) & live[:, None, :]
    earlier = jnp.arange(slots)[None, :, None] > jnp.arange(slots)[None, None, :]
    first = (live & ~jnp.any(same & earlier, axis=2)).astype(jnp.int32)
    used = jnp.any(
        (kinds[:, :, None] == jnp.arange(kinds_n, dtype=jnp.int32)[None, None, :]) & live[:, :, None], axis=1
    )
    lower = jnp.arange(kinds_n)[:, None] > jnp.arange(kinds_n)[None, :]
    lead = (used & ~jnp.any(used[:, None, :] & lower[None], axis=2)).astype(jnp.int32)
    moved = moved_blocks(
        group_rows, own_rows, energy, in_group.reshape(-1), counts, kinds.reshape(-1),
        first.reshape(-1), used.astype(jnp.int32).reshape(-1), lead.reshape(-1), coupling_blocks,
    ).reshape(blocks * block_rows, rank_cols)
    moved_gram = lax.dot_general(moved, moved, contract_rows, preferred_element_type=jnp.float32)
    cross_gram = lax.dot_general(moved, bathed, contract_rows, preferred_element_type=jnp.float32)
    local_gram = jnp.concatenate(
        [
            jnp.concatenate([moved_gram, cross_gram], axis=1),
            jnp.concatenate([cross_gram.T, bath_gram], axis=1),
        ],
        axis=0,
    )
    devices = lax.axis_size("row") * col_count
    stage_bits = devices.bit_length() - 1
    if stage_bits == 7:
        fields = [(4, 2), (0, 16), (5, 4)]
    else:
        fields = [(s, 2) for s in range(stage_bits)]
    gram_sum = kernel_sum(local_gram, fields, col_count)
    rotation = orthonormal_steps(gram_sum, rank_cols).astype(jnp.bfloat16)
    product = jnp.dot(moved, rotation[:rank_cols], preferred_element_type=jnp.float32)
    product += jnp.dot(bathed, rotation[rank_cols:], preferred_element_type=jnp.float32)
    return product.astype(jnp.bfloat16)


def solution(mesh):
    placed = (
        P(("row", "col"), None),
        P(("row", "col")),
        P(("row", "col"), None),
        P(("row", "col")),
        P(("row", "col"), None),
        P(),
        P(("row", "col")),
        P(),
    )
    return jax.shard_map(
        shards, mesh=mesh, in_specs=placed, out_specs=P(("row", "col"), None), check_vma=False
    )
```

```python
import functools

import jax
import jax.numpy as jnp
from jax import lax
from jax.experimental import pallas as pl
from jax.experimental.pallas import tpu as pltpu
from jax.sharding import PartitionSpec as P

SWEEPS = 2


time_step = 0.25


def orthonormal_steps(gram, rank_cols):
    def sweep(_, basis):
        image = jnp.dot(gram, basis, precision=lax.Precision.HIGHEST)
        inner = jnp.dot(image.T, image, precision=lax.Precision.HIGHEST)
        factor = jnp.linalg.cholesky(inner)
        return lax.linalg.triangular_solve(
            factor, image, left_side=False, lower=True, transpose_a=True
        )

    return lax.fori_loop(0, SWEEPS, sweep, jnp.eye(2 * rank_cols, rank_cols, dtype=jnp.float32))


def step_kernel(slots, ids_ref, cnt_ref, kind_ref,
                group_hbm, own_ref, ons_ref, cpl_ref, out_ref, buf, sems, acc):
    b = pl.program_id(0)
    last = pl.num_programs(0) - 1
    rank_cols = own_ref.shape[2]

    def fetch(blk, slot):
        for k in range(slots):
            @pl.when(k < cnt_ref[blk])
            def _():
                pltpu.make_async_copy(
                    group_hbm.at[ids_ref[blk * slots + k]], buf.at[slot, k], sems.at[slot, k]
                ).start()

    @pl.when(b == 0)
    def _():
        fetch(0, 0)

    @pl.when(b < last)
    def _():
        fetch(b + 1, (b + 1) % 2)

    slot = b % 2
    acc[...] = jnp.zeros_like(acc)
    for k in range(slots):
        @pl.when(k < cnt_ref[b])
        def _():
            pltpu.make_async_copy(group_hbm.at[0], buf.at[slot, k], sems.at[slot, k]).wait()
            t = kind_ref[b * slots + k]
            acc[t] += buf[slot, k].astype(jnp.float32)

    coupled = jnp.dot(cpl_ref[0], acc[0].astype(jnp.bfloat16), preferred_element_type=jnp.float32)
    for t in range(1, cpl_ref.shape[0]):
        coupled += jnp.dot(cpl_ref[t], acc[t].astype(jnp.bfloat16), preferred_element_type=jnp.float32)
    own = own_ref[0]
    wide = own.astype(jnp.float32)
    moved = wide - time_step * (ons_ref[0] * wide + coupled)
    out_ref[0] = moved.astype(out_ref.dtype)


def moved_blocks(group_rows, own_rows, energy, ids, counts, kinds, coupling_blocks):
    blocks, block_rows, rank_cols = own_rows.shape
    slots = ids.shape[0] // blocks
    kinds_n = coupling_blocks.shape[0]
    grid_spec = pltpu.PrefetchScalarGridSpec(
        num_scalar_prefetch=3,
        grid=(blocks,),
        in_specs=[
            pl.BlockSpec(memory_space=pl.ANY),
            pl.BlockSpec((1, block_rows, rank_cols), lambda b, *_: (b, 0, 0)),
            pl.BlockSpec((1, block_rows, 1), lambda b, *_: (b, 0, 0)),
            pl.BlockSpec((kinds_n, block_rows, block_rows), lambda b, *_: (0, 0, 0)),
        ],
        out_specs=pl.BlockSpec((1, block_rows, rank_cols), lambda b, *_: (b, 0, 0)),
        scratch_shapes=[
            pltpu.VMEM((2, slots, block_rows, rank_cols), group_rows.dtype),
            pltpu.SemaphoreType.DMA((2, slots)),
            pltpu.VMEM((kinds_n, block_rows, rank_cols), jnp.float32),
        ],
    )
    return pl.pallas_call(
        functools.partial(step_kernel, slots),
        grid_spec=grid_spec,
        out_shape=jax.ShapeDtypeStruct((blocks, block_rows, rank_cols), jnp.bfloat16),
        compiler_params=pltpu.CompilerParams(dimension_semantics=("arbitrary",)),
    )(ids, counts, kinds, group_rows, own_rows, energy, coupling_blocks)


def allreduce_kernel(fields, cols, x_ref, o_ref, *scratch):
    stages = len(fields)
    recv_bufs = scratch[:stages]
    send_sems, recv_sems, work = scratch[stages], scratch[stages + 1], scratch[stages + 2]
    me = lax.axis_index("row") * cols + lax.axis_index("col")

    def field(s, r):
        return (me // (1 << s)) % r

    def place(s, r, d):
        other = me + ((field(s, r) + d) % r - field(s, r)) * (1 << s)
        return (other // cols, other % cols)

    barrier = pltpu.get_barrier_semaphore()
    partners = 0
    for s, r in fields:
        for d in range(1, r):
            pl.semaphore_signal(barrier, inc=1, device_id=place(s, r, d), device_id_type=pl.DeviceIdType.MESH)
            partners += 1
    pl.semaphore_wait(barrier, partners)

    base = 0
    size = x_ref.shape[0]
    slot = 0
    for j, (s, r) in enumerate(fields):
        part = size // r
        f = field(s, r)
        src = x_ref if j == 0 else work
        copies = []
        for d in range(1, r):
            give = pl.multiple_of(base + ((f + d) % r) * part, 8)
            copy = pltpu.make_async_remote_copy(
                src_ref=src.at[pl.ds(give, part)],
                dst_ref=recv_bufs[j].at[d - 1],
                send_sem=send_sems.at[slot],
                recv_sem=recv_sems.at[slot],
                device_id=place(s, r, d),
                device_id_type=pl.DeviceIdType.MESH,
            )
            copy.start()
            copies.append(copy)
            slot += 1
        for copy in copies:
            copy.wait()
        keep = pl.multiple_of(base + f * part, 8)
        total = src[pl.ds(keep, part)]
        for d in range(1, r):
            total = total + recv_bufs[j][d - 1]
        work[pl.ds(keep, part)] = total
        base, size = keep, part
    o_ref[pl.ds(base, size)] = work[pl.ds(base, size)]
    for j in reversed(range(stages)):
        s, r = fields[j]
        block = o_ref.at[pl.ds(base, size)]
        copies = []
        for d in range(1, r):
            copy = pltpu.make_async_remote_copy(
                src_ref=block,
                dst_ref=block,
                send_sem=send_sems.at[slot],
                recv_sem=recv_sems.at[slot],
                device_id=place(s, r, d),
                device_id_type=pl.DeviceIdType.MESH,
            )
            copy.start()
            copies.append(copy)
            slot += 1
        for copy in copies:
            copy.wait()
        base = pl.multiple_of(base - field(s, r) * size, 8)
        size = size * r


def kernel_sum(local, fields, cols, channel):
    lanes = 128
    flat = local.reshape(-1, lanes)
    rows = flat.shape[0]
    scratch = []
    left = rows
    for s, r in fields:
        left //= r
        scratch.append(pltpu.VMEM((r - 1, left, lanes), jnp.float32))
    copies = 2 * sum(r - 1 for _, r in fields)
    scratch += [pltpu.SemaphoreType.DMA((copies,)), pltpu.SemaphoreType.DMA((copies,))]
    scratch += [pltpu.VMEM(flat.shape, jnp.float32)]
    total = pl.pallas_call(
        functools.partial(allreduce_kernel, tuple(fields), cols),
        out_shape=jax.ShapeDtypeStruct(flat.shape, flat.dtype),
        in_specs=[pl.BlockSpec(memory_space=pltpu.VMEM)],
        out_specs=pl.BlockSpec(memory_space=pltpu.VMEM),
        scratch_shapes=scratch,
        compiler_params=pltpu.CompilerParams(collective_id=channel, has_side_effects=True),
    )(flat)
    return total.reshape(local.shape)


def shards(
    density_factor,
    onsite,
    neighbour_ids,
    neighbour_count,
    coupling_type,
    coupling_blocks,
    bath_pattern,
    bath_blocks,
):
    blocks, slots = neighbour_ids.shape
    block_rows = coupling_blocks.shape[1]
    rank_cols = density_factor.shape[1]
    col_count = lax.axis_size("col")
    group_blocks = col_count * blocks
    row_place = lax.axis_index("row")
    in_group = jnp.clip(neighbour_ids - row_place * group_blocks, 0, group_blocks - 1)
    counts = jnp.clip(neighbour_count, 1, slots)
    kinds = jnp.clip(coupling_type, 0, coupling_blocks.shape[0] - 1)
    bath_kind = jnp.clip(bath_pattern, 0, bath_blocks.shape[0] - 1)
    own_rows = density_factor.reshape(blocks, block_rows, rank_cols)
    bathed = jnp.einsum(
        "bij,bjr->bir", bath_blocks[bath_kind], own_rows, preferred_element_type=jnp.float32
    ).astype(jnp.bfloat16).reshape(blocks * block_rows, rank_cols)
    contract_rows = (((0,), (0,)), ((), ()))
    bath_gram = lax.dot_general(bathed, bathed, contract_rows, preferred_element_type=jnp.float32)
    devices = lax.axis_size("row") * col_count
    stage_bits = devices.bit_length() - 1
    if stage_bits == 7:
        fields = [(4, 2), (0, 16), (5, 4)]
    else:
        fields = [(s, 2) for s in range(stage_bits)]
    bath_flat = bath_gram.reshape(-1, 128)
    bath_flat = jnp.concatenate([bath_flat, jnp.zeros_like(bath_flat)], axis=0)
    bath_sum = kernel_sum(bath_flat, fields, col_count, 1)[: bath_flat.shape[0] // 2]
    bath_sum = bath_sum.reshape(bath_gram.shape)
    gathered = lax.all_gather(density_factor, "col", axis=0, tiled=True)
    group_rows = gathered.reshape(group_blocks, block_rows, rank_cols)
    energy = onsite.reshape(blocks, block_rows, 1)
    moved = moved_blocks(
        group_rows, own_rows, energy, in_group.reshape(-1), counts, kinds.reshape(-1), coupling_blocks,
    ).reshape(blocks * block_rows, rank_cols)
    moved_gram = lax.dot_general(moved, moved, contract_rows, preferred_element_type=jnp.float32)
    cross_gram = lax.dot_general(moved, bathed, contract_rows, preferred_element_type=jnp.float32)
    upper = kernel_sum(jnp.concatenate([moved_gram, cross_gram], axis=0), fields, col_count, 0)
    moved_sum, cross_sum = upper[:rank_cols], upper[rank_cols:]
    gram_sum = jnp.concatenate(
        [
            jnp.concatenate([moved_sum, cross_sum], axis=1),
            jnp.concatenate([cross_sum.T, bath_sum], axis=1),
        ],
        axis=0,
    )
    rotation = orthonormal_steps(gram_sum, rank_cols).astype(jnp.bfloat16)
    product = jnp.dot(moved, rotation[:rank_cols], preferred_element_type=jnp.float32)
    product += jnp.dot(bathed, rotation[rank_cols:], preferred_element_type=jnp.float32)
    return product.astype(jnp.bfloat16)


def solution(mesh):
    placed = (
        P(("row", "col"), None),
        P(("row", "col")),
        P(("row", "col"), None),
        P(("row", "col")),
        P(("row", "col"), None),
        P(),
        P(("row", "col")),
        P(),
    )
    return jax.shard_map(
        shards, mesh=mesh, in_specs=placed, out_specs=P(("row", "col"), None), check_vma=False
    )
```

```python
import functools

import jax
import jax.numpy as jnp
from jax import lax
from jax.experimental import pallas as pl
from jax.experimental.pallas import tpu as pltpu
from jax.sharding import PartitionSpec as P

SWEEPS = 2


time_step = 0.25


def orthonormal_steps(gram, rank_cols):
    def sweep(_, basis):
        image = jnp.dot(gram, basis, precision=lax.Precision.HIGHEST)
        inner = jnp.dot(image.T, image, precision=lax.Precision.HIGHEST)
        factor = jnp.linalg.cholesky(inner)
        return lax.linalg.triangular_solve(
            factor, image, left_side=False, lower=True, transpose_a=True
        )

    return lax.fori_loop(0, SWEEPS, sweep, jnp.eye(2 * rank_cols, rank_cols, dtype=jnp.float32))


def step_kernel(slots, ids_ref, cnt_ref, kind_ref,
                group_hbm, own_ref, ons_ref, cpl_ref, out_ref, buf, sems, acc):
    b = pl.program_id(0)
    last = pl.num_programs(0) - 1
    rank_cols = own_ref.shape[2]

    def fetch(blk, slot):
        for k in range(slots):
            @pl.when(k < cnt_ref[blk])
            def _():
                pltpu.make_async_copy(
                    group_hbm.at[ids_ref[blk * slots + k]], buf.at[slot, k], sems.at[slot, k]
                ).start()

    @pl.when(b == 0)
    def _():
        fetch(0, 0)

    @pl.when(b < last)
    def _():
        fetch(b + 1, (b + 1) % 2)

    slot = b % 2
    acc[...] = jnp.zeros_like(acc)
    for k in range(slots):
        @pl.when(k < cnt_ref[b])
        def _():
            pltpu.make_async_copy(group_hbm.at[0], buf.at[slot, k], sems.at[slot, k]).wait()
            t = kind_ref[b * slots + k]
            acc[t] += buf[slot, k].astype(jnp.float32)

    coupled = jnp.dot(cpl_ref[0], acc[0].astype(jnp.bfloat16), preferred_element_type=jnp.float32)
    for t in range(1, cpl_ref.shape[0]):
        coupled += jnp.dot(cpl_ref[t], acc[t].astype(jnp.bfloat16), preferred_element_type=jnp.float32)
    own = own_ref[0]
    wide = own.astype(jnp.float32)
    moved = wide - time_step * (ons_ref[0] * wide + coupled)
    out_ref[0] = moved.astype(out_ref.dtype)


def moved_blocks(group_rows, own_rows, energy, ids, counts, kinds, coupling_blocks):
    blocks, block_rows, rank_cols = own_rows.shape
    slots = ids.shape[0] // blocks
    kinds_n = coupling_blocks.shape[0]
    grid_spec = pltpu.PrefetchScalarGridSpec(
        num_scalar_prefetch=3,
        grid=(blocks,),
        in_specs=[
            pl.BlockSpec(memory_space=pl.ANY),
            pl.BlockSpec((1, block_rows, rank_cols), lambda b, *_: (b, 0, 0)),
            pl.BlockSpec((1, block_rows, 1), lambda b, *_: (b, 0, 0)),
            pl.BlockSpec((kinds_n, block_rows, block_rows), lambda b, *_: (0, 0, 0)),
        ],
        out_specs=pl.BlockSpec((1, block_rows, rank_cols), lambda b, *_: (b, 0, 0)),
        scratch_shapes=[
            pltpu.VMEM((2, slots, block_rows, rank_cols), group_rows.dtype),
            pltpu.SemaphoreType.DMA((2, slots)),
            pltpu.VMEM((kinds_n, block_rows, rank_cols), jnp.float32),
        ],
    )
    return pl.pallas_call(
        functools.partial(step_kernel, slots),
        grid_spec=grid_spec,
        out_shape=jax.ShapeDtypeStruct((blocks, block_rows, rank_cols), jnp.bfloat16),
        compiler_params=pltpu.CompilerParams(dimension_semantics=("arbitrary",)),
    )(ids, counts, kinds, group_rows, own_rows, energy, coupling_blocks)


def allreduce_kernel(fields, cols, x_ref, o_ref, *scratch):
    stages = len(fields)
    recv_bufs = scratch[:stages]
    send_sems, recv_sems, work = scratch[stages], scratch[stages + 1], scratch[stages + 2]
    me = lax.axis_index("row") * cols + lax.axis_index("col")

    def field(s, r):
        return (me // (1 << s)) % r

    def place(s, r, d):
        other = me + ((field(s, r) + d) % r - field(s, r)) * (1 << s)
        return (other // cols, other % cols)

    barrier = pltpu.get_barrier_semaphore()
    partners = 0
    for s, r in fields:
        for d in range(1, r):
            pl.semaphore_signal(barrier, inc=1, device_id=place(s, r, d), device_id_type=pl.DeviceIdType.MESH)
            partners += 1
    pl.semaphore_wait(barrier, partners)

    base = 0
    size = x_ref.shape[0]
    slot = 0
    for j, (s, r) in enumerate(fields):
        part = size // r
        f = field(s, r)
        src = x_ref if j == 0 else work
        copies = []
        for d in range(1, r):
            give = pl.multiple_of(base + ((f + d) % r) * part, 8)
            copy = pltpu.make_async_remote_copy(
                src_ref=src.at[pl.ds(give, part)],
                dst_ref=recv_bufs[j].at[d - 1],
                send_sem=send_sems.at[slot],
                recv_sem=recv_sems.at[slot],
                device_id=place(s, r, d),
                device_id_type=pl.DeviceIdType.MESH,
            )
            copy.start()
            copies.append(copy)
            slot += 1
        for copy in copies:
            copy.wait()
        keep = pl.multiple_of(base + f * part, 8)
        total = src[pl.ds(keep, part)]
        for d in range(1, r):
            total = total + recv_bufs[j][d - 1]
        work[pl.ds(keep, part)] = total
        base, size = keep, part
    o_ref[pl.ds(base, size)] = work[pl.ds(base, size)]
    for j in reversed(range(stages)):
        s, r = fields[j]
        block = o_ref.at[pl.ds(base, size)]
        copies = []
        for d in range(1, r):
            copy = pltpu.make_async_remote_copy(
                src_ref=block,
                dst_ref=block,
                send_sem=send_sems.at[slot],
                recv_sem=recv_sems.at[slot],
                device_id=place(s, r, d),
                device_id_type=pl.DeviceIdType.MESH,
            )
            copy.start()
            copies.append(copy)
            slot += 1
        for copy in copies:
            copy.wait()
        base = pl.multiple_of(base - field(s, r) * size, 8)
        size = size * r


def kernel_sum(local, fields, cols, channel):
    lanes = 128
    flat = local.reshape(-1, lanes)
    rows = flat.shape[0]
    scratch = []
    left = rows
    for s, r in fields:
        left //= r
        scratch.append(pltpu.VMEM((r - 1, left, lanes), jnp.float32))
    copies = 2 * sum(r - 1 for _, r in fields)
    scratch += [pltpu.SemaphoreType.DMA((copies,)), pltpu.SemaphoreType.DMA((copies,))]
    scratch += [pltpu.VMEM(flat.shape, jnp.float32)]
    total = pl.pallas_call(
        functools.partial(allreduce_kernel, tuple(fields), cols),
        out_shape=jax.ShapeDtypeStruct(flat.shape, flat.dtype),
        in_specs=[pl.BlockSpec(memory_space=pltpu.VMEM)],
        out_specs=pl.BlockSpec(memory_space=pltpu.VMEM),
        scratch_shapes=scratch,
        compiler_params=pltpu.CompilerParams(collective_id=channel, has_side_effects=True),
    )(flat)
    return total.reshape(local.shape)


def shards(
    density_factor,
    onsite,
    neighbour_ids,
    neighbour_count,
    coupling_type,
    coupling_blocks,
    bath_pattern,
    bath_blocks,
):
    blocks, slots = neighbour_ids.shape
    block_rows = coupling_blocks.shape[1]
    rank_cols = density_factor.shape[1]
    col_count = lax.axis_size("col")
    group_blocks = col_count * blocks
    row_place = lax.axis_index("row")
    in_group = jnp.clip(neighbour_ids - row_place * group_blocks, 0, group_blocks - 1)
    counts = jnp.clip(neighbour_count, 1, slots)
    kinds = jnp.clip(coupling_type, 0, coupling_blocks.shape[0] - 1)
    bath_kind = jnp.clip(bath_pattern, 0, bath_blocks.shape[0] - 1)
    own_rows = density_factor.reshape(blocks, block_rows, rank_cols)
    bathed = jnp.einsum(
        "bij,bjr->bir", bath_blocks[bath_kind], own_rows, preferred_element_type=jnp.float32
    ).astype(jnp.bfloat16).reshape(blocks * block_rows, rank_cols)
    contract_rows = (((0,), (0,)), ((), ()))
    bath_gram = lax.dot_general(bathed, bathed, contract_rows, preferred_element_type=jnp.float32)
    devices = lax.axis_size("row") * col_count
    stage_bits = devices.bit_length() - 1
    if stage_bits == 7:
        fields = [(4, 2), (0, 16), (5, 4)]
    else:
        fields = [(s, 2) for s in range(stage_bits)]
    bath_flat = bath_gram.reshape(-1, 128)
    bath_flat = jnp.concatenate([bath_flat, jnp.zeros_like(bath_flat)], axis=0)
    bath_sum = kernel_sum(bath_flat, fields, col_count, 1)[: bath_flat.shape[0] // 2]
    bath_sum = bath_sum.reshape(bath_gram.shape)
    gathered = lax.all_gather(density_factor, "col", axis=0, tiled=True)
    group_rows = gathered.reshape(group_blocks, block_rows, rank_cols)
    energy = onsite.reshape(blocks, block_rows, 1)
    moved = moved_blocks(
        group_rows, own_rows, energy, in_group.reshape(-1), counts, kinds.reshape(-1), coupling_blocks,
    ).reshape(blocks * block_rows, rank_cols)
    moved_gram = lax.dot_general(moved, moved, contract_rows, preferred_element_type=jnp.float32)
    cross_gram = lax.dot_general(moved, bathed, contract_rows, preferred_element_type=jnp.float32)
    late_fields = [(4, 2), (5, 4), (0, 16)] if stage_bits == 7 else fields
    upper = kernel_sum(jnp.concatenate([moved_gram, cross_gram], axis=0), late_fields, col_count, 0)
    moved_sum, cross_sum = upper[:rank_cols], upper[rank_cols:]
    gram_sum = jnp.concatenate(
        [
            jnp.concatenate([moved_sum, cross_sum], axis=1),
            jnp.concatenate([cross_sum.T, bath_sum], axis=1),
        ],
        axis=0,
    )
    rotation = orthonormal_steps(gram_sum, rank_cols).astype(jnp.bfloat16)
    product = jnp.dot(moved, rotation[:rank_cols], preferred_element_type=jnp.float32)
    product += jnp.dot(bathed, rotation[rank_cols:], preferred_element_type=jnp.float32)
    return product.astype(jnp.bfloat16)


def solution(mesh):
    placed = (
        P(("row", "col"), None),
        P(("row", "col")),
        P(("row", "col"), None),
        P(("row", "col")),
        P(("row", "col"), None),
        P(),
        P(("row", "col")),
        P(),
    )
    return jax.shard_map(
        shards, mesh=mesh, in_specs=placed, out_specs=P(("row", "col"), None), check_vma=False
    )
```

```python
import functools

import jax
import jax.numpy as jnp
from jax import lax
from jax.experimental import pallas as pl
from jax.experimental.pallas import tpu as pltpu
from jax.sharding import PartitionSpec as P

SWEEPS = 2


time_step = 0.25


def orthonormal_steps(gram, rank_cols):
    def sweep(_, basis):
        image = jnp.dot(gram, basis, precision=lax.Precision.HIGHEST)
        inner = jnp.dot(image.T, image, precision=lax.Precision.HIGHEST)
        factor = jnp.linalg.cholesky(inner)
        return lax.linalg.triangular_solve(
            factor, image, left_side=False, lower=True, transpose_a=True
        )

    return lax.fori_loop(0, SWEEPS, sweep, jnp.eye(2 * rank_cols, rank_cols, dtype=jnp.float32))


def step_kernel(slots, ids_ref, cnt_ref, kind_ref,
                group_hbm, own_ref, ons_ref, cpl_ref, out_ref, buf, sems, acc):
    b = pl.program_id(0)
    last = pl.num_programs(0) - 1
    rank_cols = own_ref.shape[2]

    def fetch(blk, slot):
        for k in range(slots):
            @pl.when(k < cnt_ref[blk])
            def _():
                pltpu.make_async_copy(
                    group_hbm.at[ids_ref[blk * slots + k]], buf.at[slot, k], sems.at[slot, k]
                ).start()

    @pl.when(b == 0)
    def _():
        fetch(0, 0)

    @pl.when(b < last)
    def _():
        fetch(b + 1, (b + 1) % 2)

    slot = b % 2
    acc[...] = jnp.zeros_like(acc)
    for k in range(slots):
        @pl.when(k < cnt_ref[b])
        def _():
            pltpu.make_async_copy(group_hbm.at[0], buf.at[slot, k], sems.at[slot, k]).wait()
            t = kind_ref[b * slots + k]
            acc[t] += buf[slot, k].astype(jnp.float32)

    coupled = jnp.dot(cpl_ref[0], acc[0].astype(jnp.bfloat16), preferred_element_type=jnp.float32)
    for t in range(1, cpl_ref.shape[0]):
        coupled += jnp.dot(cpl_ref[t], acc[t].astype(jnp.bfloat16), preferred_element_type=jnp.float32)
    own = own_ref[0]
    wide = own.astype(jnp.float32)
    moved = wide - time_step * (ons_ref[0] * wide + coupled)
    out_ref[0] = moved.astype(out_ref.dtype)


def moved_blocks(group_rows, own_rows, energy, ids, counts, kinds, coupling_blocks):
    blocks, block_rows, rank_cols = own_rows.shape
    slots = ids.shape[0] // blocks
    kinds_n = coupling_blocks.shape[0]
    grid_spec = pltpu.PrefetchScalarGridSpec(
        num_scalar_prefetch=3,
        grid=(blocks,),
        in_specs=[
            pl.BlockSpec(memory_space=pl.ANY),
            pl.BlockSpec((1, block_rows, rank_cols), lambda b, *_: (b, 0, 0)),
            pl.BlockSpec((1, block_rows, 1), lambda b, *_: (b, 0, 0)),
            pl.BlockSpec((kinds_n, block_rows, block_rows), lambda b, *_: (0, 0, 0)),
        ],
        out_specs=pl.BlockSpec((1, block_rows, rank_cols), lambda b, *_: (b, 0, 0)),
        scratch_shapes=[
            pltpu.VMEM((2, slots, block_rows, rank_cols), group_rows.dtype),
            pltpu.SemaphoreType.DMA((2, slots)),
            pltpu.VMEM((kinds_n, block_rows, rank_cols), jnp.float32),
        ],
    )
    return pl.pallas_call(
        functools.partial(step_kernel, slots),
        grid_spec=grid_spec,
        out_shape=jax.ShapeDtypeStruct((blocks, block_rows, rank_cols), jnp.bfloat16),
        compiler_params=pltpu.CompilerParams(dimension_semantics=("arbitrary",)),
    )(ids, counts, kinds, group_rows, own_rows, energy, coupling_blocks)


def allreduce_kernel(fields, cols, x_ref, o_ref, *scratch):
    stages = len(fields)
    recv_bufs = scratch[:stages]
    send_sems, recv_sems, work = scratch[stages], scratch[stages + 1], scratch[stages + 2]
    me = lax.axis_index("row") * cols + lax.axis_index("col")

    def field(s, r):
        return (me // (1 << s)) % r

    def place(s, r, d):
        other = me + ((field(s, r) + d) % r - field(s, r)) * (1 << s)
        return (other // cols, other % cols)

    barrier = pltpu.get_barrier_semaphore()
    partners = 0
    for s, r in fields:
        for d in range(1, r):
            pl.semaphore_signal(barrier, inc=1, device_id=place(s, r, d), device_id_type=pl.DeviceIdType.MESH)
            partners += 1
    pl.semaphore_wait(barrier, partners)

    base = 0
    size = x_ref.shape[0]
    slot = 0
    for j, (s, r) in enumerate(fields):
        part = size // r
        f = field(s, r)
        src = x_ref if j == 0 else work
        copies = []
        for d in range(1, r):
            give = pl.multiple_of(base + ((f + d) % r) * part, 8)
            copy = pltpu.make_async_remote_copy(
                src_ref=src.at[pl.ds(give, part)],
                dst_ref=recv_bufs[j].at[d - 1],
                send_sem=send_sems.at[slot],
                recv_sem=recv_sems.at[slot],
                device_id=place(s, r, d),
                device_id_type=pl.DeviceIdType.MESH,
            )
            copy.start()
            copies.append(copy)
            slot += 1
        for copy in copies:
            copy.wait()
        keep = pl.multiple_of(base + f * part, 8)
        total = src[pl.ds(keep, part)]
        for d in range(1, r):
            total = total + recv_bufs[j][d - 1]
        work[pl.ds(keep, part)] = total
        base, size = keep, part
    o_ref[pl.ds(base, size)] = work[pl.ds(base, size)]
    for j in reversed(range(stages)):
        s, r = fields[j]
        block = o_ref.at[pl.ds(base, size)]
        copies = []
        for d in range(1, r):
            copy = pltpu.make_async_remote_copy(
                src_ref=block,
                dst_ref=block,
                send_sem=send_sems.at[slot],
                recv_sem=recv_sems.at[slot],
                device_id=place(s, r, d),
                device_id_type=pl.DeviceIdType.MESH,
            )
            copy.start()
            copies.append(copy)
            slot += 1
        for copy in copies:
            copy.wait()
        base = pl.multiple_of(base - field(s, r) * size, 8)
        size = size * r


def kernel_sum(local, fields, cols, channel):
    lanes = 128
    flat = local.reshape(-1, lanes)
    rows = flat.shape[0]
    scratch = []
    left = rows
    for s, r in fields:
        left //= r
        scratch.append(pltpu.VMEM((r - 1, left, lanes), jnp.float32))
    copies = 2 * sum(r - 1 for _, r in fields)
    scratch += [pltpu.SemaphoreType.DMA((copies,)), pltpu.SemaphoreType.DMA((copies,))]
    scratch += [pltpu.VMEM(flat.shape, jnp.float32)]
    total = pl.pallas_call(
        functools.partial(allreduce_kernel, tuple(fields), cols),
        out_shape=jax.ShapeDtypeStruct(flat.shape, flat.dtype),
        in_specs=[pl.BlockSpec(memory_space=pltpu.VMEM)],
        out_specs=pl.BlockSpec(memory_space=pltpu.VMEM),
        scratch_shapes=scratch,
        compiler_params=pltpu.CompilerParams(collective_id=channel, has_side_effects=True),
    )(flat)
    return total.reshape(local.shape)


def shards(
    density_factor,
    onsite,
    neighbour_ids,
    neighbour_count,
    coupling_type,
    coupling_blocks,
    bath_pattern,
    bath_blocks,
):
    blocks, slots = neighbour_ids.shape
    block_rows = coupling_blocks.shape[1]
    rank_cols = density_factor.shape[1]
    col_count = lax.axis_size("col")
    group_blocks = col_count * blocks
    row_place = lax.axis_index("row")
    in_group = jnp.clip(neighbour_ids - row_place * group_blocks, 0, group_blocks - 1)
    counts = jnp.clip(neighbour_count, 1, slots)
    kinds = jnp.clip(coupling_type, 0, coupling_blocks.shape[0] - 1)
    bath_kind = jnp.clip(bath_pattern, 0, bath_blocks.shape[0] - 1)
    own_rows = density_factor.reshape(blocks, block_rows, rank_cols)
    bathed = jnp.einsum(
        "bij,bjr->bir", bath_blocks[bath_kind], own_rows, preferred_element_type=jnp.float32
    ).astype(jnp.bfloat16).reshape(blocks * block_rows, rank_cols)
    contract_rows = (((0,), (0,)), ((), ()))
    bath_gram = lax.dot_general(bathed, bathed, contract_rows, preferred_element_type=jnp.float32)
    devices = lax.axis_size("row") * col_count
    stage_bits = devices.bit_length() - 1
    if stage_bits == 7:
        fields = [(4, 2), (0, 16), (5, 4)]
    else:
        fields = [(s, 2) for s in range(stage_bits)]
    bath_flat = bath_gram.reshape(-1, 128)
    bath_flat = jnp.concatenate([bath_flat, jnp.zeros_like(bath_flat)], axis=0)
    early_fields = [(4, 2), (5, 4), (0, 16)] if stage_bits == 7 else fields
    bath_sum = kernel_sum(bath_flat, early_fields, col_count, 1)[: bath_flat.shape[0] // 2]
    bath_sum = bath_sum.reshape(bath_gram.shape)
    gathered = lax.all_gather(density_factor, "col", axis=0, tiled=True)
    group_rows = gathered.reshape(group_blocks, block_rows, rank_cols)
    energy = onsite.reshape(blocks, block_rows, 1)
    moved = moved_blocks(
        group_rows, own_rows, energy, in_group.reshape(-1), counts, kinds.reshape(-1), coupling_blocks,
    ).reshape(blocks * block_rows, rank_cols)
    moved_gram = lax.dot_general(moved, moved, contract_rows, preferred_element_type=jnp.float32)
    cross_gram = lax.dot_general(moved, bathed, contract_rows, preferred_element_type=jnp.float32)
    upper = kernel_sum(jnp.concatenate([moved_gram, cross_gram], axis=0), fields, col_count, 0)
    moved_sum, cross_sum = upper[:rank_cols], upper[rank_cols:]
    gram_sum = jnp.concatenate(
        [
            jnp.concatenate([moved_sum, cross_sum], axis=1),
            jnp.concatenate([cross_sum.T, bath_sum], axis=1),
        ],
        axis=0,
    )
    rotation = orthonormal_steps(gram_sum, rank_cols).astype(jnp.bfloat16)
    product = jnp.dot(moved, rotation[:rank_cols], preferred_element_type=jnp.float32)
    product += jnp.dot(bathed, rotation[rank_cols:], preferred_element_type=jnp.float32)
    return product.astype(jnp.bfloat16)


def solution(mesh):
    placed = (
        P(("row", "col"), None),
        P(("row", "col")),
        P(("row", "col"), None),
        P(("row", "col")),
        P(("row", "col"), None),
        P(),
        P(("row", "col")),
        P(),
    )
    return jax.shard_map(
        shards, mesh=mesh, in_specs=placed, out_specs=P(("row", "col"), None), check_vma=False
    )
```

```python
import functools

import jax
import jax.numpy as jnp
from jax import lax
from jax.experimental import pallas as pl
from jax.experimental.pallas import tpu as pltpu
from jax.sharding import PartitionSpec as P

SWEEPS = 2


time_step = 0.25


def orthonormal_steps(gram, rank_cols):
    def sweep(_, basis):
        image = jnp.dot(gram, basis, precision=lax.Precision.HIGHEST)
        inner = jnp.dot(image.T, image, precision=lax.Precision.HIGHEST)
        factor = jnp.linalg.cholesky(inner)
        return lax.linalg.triangular_solve(
            factor, image, left_side=False, lower=True, transpose_a=True
        )

    return lax.fori_loop(0, SWEEPS, sweep, jnp.eye(2 * rank_cols, rank_cols, dtype=jnp.float32))


def step_kernel(slots, ids_ref, cnt_ref, kind_ref,
                group_hbm, own_ref, ons_ref, cpl_ref, out_ref, buf, sems, acc):
    b = pl.program_id(0)
    last = pl.num_programs(0) - 1
    rank_cols = own_ref.shape[2]

    def fetch(blk, slot):
        for k in range(slots):
            @pl.when(k < cnt_ref[blk])
            def _():
                pltpu.make_async_copy(
                    group_hbm.at[ids_ref[blk * slots + k]], buf.at[slot, k], sems.at[slot, k]
                ).start()

    @pl.when(b == 0)
    def _():
        fetch(0, 0)

    @pl.when(b < last)
    def _():
        fetch(b + 1, (b + 1) % 2)

    slot = b % 2
    acc[...] = jnp.zeros_like(acc)
    for k in range(slots):
        @pl.when(k < cnt_ref[b])
        def _():
            pltpu.make_async_copy(group_hbm.at[0], buf.at[slot, k], sems.at[slot, k]).wait()
            t = kind_ref[b * slots + k]
            acc[t] += buf[slot, k].astype(jnp.float32)

    coupled = jnp.dot(cpl_ref[0], acc[0].astype(jnp.bfloat16), preferred_element_type=jnp.float32)
    for t in range(1, cpl_ref.shape[0]):
        coupled += jnp.dot(cpl_ref[t], acc[t].astype(jnp.bfloat16), preferred_element_type=jnp.float32)
    own = own_ref[0]
    wide = own.astype(jnp.float32)
    moved = wide - time_step * (ons_ref[0] * wide + coupled)
    out_ref[0] = moved.astype(out_ref.dtype)


def moved_blocks(group_rows, own_rows, energy, ids, counts, kinds, coupling_blocks):
    blocks, block_rows, rank_cols = own_rows.shape
    slots = ids.shape[0] // blocks
    kinds_n = coupling_blocks.shape[0]
    grid_spec = pltpu.PrefetchScalarGridSpec(
        num_scalar_prefetch=3,
        grid=(blocks,),
        in_specs=[
            pl.BlockSpec(memory_space=pl.ANY),
            pl.BlockSpec((1, block_rows, rank_cols), lambda b, *_: (b, 0, 0)),
            pl.BlockSpec((1, block_rows, 1), lambda b, *_: (b, 0, 0)),
            pl.BlockSpec((kinds_n, block_rows, block_rows), lambda b, *_: (0, 0, 0)),
        ],
        out_specs=pl.BlockSpec((1, block_rows, rank_cols), lambda b, *_: (b, 0, 0)),
        scratch_shapes=[
            pltpu.VMEM((2, slots, block_rows, rank_cols), group_rows.dtype),
            pltpu.SemaphoreType.DMA((2, slots)),
            pltpu.VMEM((kinds_n, block_rows, rank_cols), jnp.float32),
        ],
    )
    return pl.pallas_call(
        functools.partial(step_kernel, slots),
        grid_spec=grid_spec,
        out_shape=jax.ShapeDtypeStruct((blocks, block_rows, rank_cols), jnp.bfloat16),
        compiler_params=pltpu.CompilerParams(dimension_semantics=("arbitrary",)),
    )(ids, counts, kinds, group_rows, own_rows, energy, coupling_blocks)


def allreduce_kernel(fields, cols, x_ref, o_ref, *scratch):
    stages = len(fields)
    recv_bufs = scratch[:stages]
    send_sems, recv_sems, work = scratch[stages], scratch[stages + 1], scratch[stages + 2]
    me = lax.axis_index("row") * cols + lax.axis_index("col")

    def field(s, r):
        return (me // (1 << s)) % r

    def place(s, r, d):
        other = me + ((field(s, r) + d) % r - field(s, r)) * (1 << s)
        return (other // cols, other % cols)

    barrier = pltpu.get_barrier_semaphore()
    partners = 0
    for s, r in fields:
        for d in range(1, r):
            pl.semaphore_signal(barrier, inc=1, device_id=place(s, r, d), device_id_type=pl.DeviceIdType.MESH)
            partners += 1
    pl.semaphore_wait(barrier, partners)

    base = 0
    size = x_ref.shape[0]
    slot = 0
    for j, (s, r) in enumerate(fields):
        part = size // r
        f = field(s, r)
        src = x_ref if j == 0 else work
        copies = []
        for d in range(1, r):
            give = pl.multiple_of(base + ((f + d) % r) * part, 8)
            copy = pltpu.make_async_remote_copy(
                src_ref=src.at[pl.ds(give, part)],
                dst_ref=recv_bufs[j].at[d - 1],
                send_sem=send_sems.at[slot],
                recv_sem=recv_sems.at[slot],
                device_id=place(s, r, d),
                device_id_type=pl.DeviceIdType.MESH,
            )
            copy.start()
            copies.append(copy)
            slot += 1
        for copy in copies:
            copy.wait()
        keep = pl.multiple_of(base + f * part, 8)
        total = src[pl.ds(keep, part)]
        for d in range(1, r):
            total = total + recv_bufs[j][d - 1]
        work[pl.ds(keep, part)] = total
        base, size = keep, part
    o_ref[pl.ds(base, size)] = work[pl.ds(base, size)]
    for j in reversed(range(stages)):
        s, r = fields[j]
        block = o_ref.at[pl.ds(base, size)]
        copies = []
        for d in range(1, r):
            copy = pltpu.make_async_remote_copy(
                src_ref=block,
                dst_ref=block,
                send_sem=send_sems.at[slot],
                recv_sem=recv_sems.at[slot],
                device_id=place(s, r, d),
                device_id_type=pl.DeviceIdType.MESH,
            )
            copy.start()
            copies.append(copy)
            slot += 1
        for copy in copies:
            copy.wait()
        base = pl.multiple_of(base - field(s, r) * size, 8)
        size = size * r


def kernel_sum(local, fields, cols, channel):
    lanes = 128
    flat = local.reshape(-1, lanes)
    rows = flat.shape[0]
    scratch = []
    left = rows
    for s, r in fields:
        left //= r
        scratch.append(pltpu.VMEM((r - 1, left, lanes), jnp.float32))
    copies = 2 * sum(r - 1 for _, r in fields)
    scratch += [pltpu.SemaphoreType.DMA((copies,)), pltpu.SemaphoreType.DMA((copies,))]
    scratch += [pltpu.VMEM(flat.shape, jnp.float32)]
    total = pl.pallas_call(
        functools.partial(allreduce_kernel, tuple(fields), cols),
        out_shape=jax.ShapeDtypeStruct(flat.shape, flat.dtype),
        in_specs=[pl.BlockSpec(memory_space=pltpu.VMEM)],
        out_specs=pl.BlockSpec(memory_space=pltpu.VMEM),
        scratch_shapes=scratch,
        compiler_params=pltpu.CompilerParams(collective_id=channel, has_side_effects=True),
    )(flat)
    return total.reshape(local.shape)


def shards(
    density_factor,
    onsite,
    neighbour_ids,
    neighbour_count,
    coupling_type,
    coupling_blocks,
    bath_pattern,
    bath_blocks,
):
    blocks, slots = neighbour_ids.shape
    block_rows = coupling_blocks.shape[1]
    rank_cols = density_factor.shape[1]
    col_count = lax.axis_size("col")
    group_blocks = col_count * blocks
    row_place = lax.axis_index("row")
    in_group = jnp.clip(neighbour_ids - row_place * group_blocks, 0, group_blocks - 1)
    counts = jnp.clip(neighbour_count, 1, slots)
    kinds = jnp.clip(coupling_type, 0, coupling_blocks.shape[0] - 1)
    bath_kind = jnp.clip(bath_pattern, 0, bath_blocks.shape[0] - 1)
    own_rows = density_factor.reshape(blocks, block_rows, rank_cols)
    bathed = jnp.einsum(
        "bij,bjr->bir", bath_blocks[bath_kind], own_rows, preferred_element_type=jnp.float32
    ).astype(jnp.bfloat16).reshape(blocks * block_rows, rank_cols)
    contract_rows = (((0,), (0,)), ((), ()))
    bath_gram = lax.dot_general(bathed, bathed, contract_rows, preferred_element_type=jnp.float32)
    devices = lax.axis_size("row") * col_count
    stage_bits = devices.bit_length() - 1
    if stage_bits == 7:
        fields = [(4, 2), (0, 16), (5, 4)]
    else:
        fields = [(s, 2) for s in range(stage_bits)]
    bath_flat = bath_gram.reshape(-1, 128)
    bath_flat = jnp.concatenate([bath_flat, jnp.zeros_like(bath_flat)], axis=0)
    early_fields = [(4, 2), (5, 4), (0, 16)] if stage_bits == 7 else fields
    bath_sum = kernel_sum(bath_flat, early_fields, col_count, 1)[: bath_flat.shape[0] // 2]
    bath_sum = bath_sum.reshape(bath_gram.shape)
    gathered = lax.all_gather(density_factor, "col", axis=0, tiled=True)
    group_rows = gathered.reshape(group_blocks, block_rows, rank_cols)
    energy = onsite.reshape(blocks, block_rows, 1)
    moved = moved_blocks(
        group_rows, own_rows, energy, in_group.reshape(-1), counts, kinds.reshape(-1), coupling_blocks,
    ).reshape(blocks * block_rows, rank_cols)
    moved_gram = lax.dot_general(moved, moved, contract_rows, preferred_element_type=jnp.float32)
    cross_gram = lax.dot_general(moved, bathed, contract_rows, preferred_element_type=jnp.float32)
    late_fields = [(4, 8), (0, 16)] if stage_bits == 7 else fields
    upper = kernel_sum(jnp.concatenate([moved_gram, cross_gram], axis=0), late_fields, col_count, 0)
    moved_sum, cross_sum = upper[:rank_cols], upper[rank_cols:]
    gram_sum = jnp.concatenate(
        [
            jnp.concatenate([moved_sum, cross_sum], axis=1),
            jnp.concatenate([cross_sum.T, bath_sum], axis=1),
        ],
        axis=0,
    )
    rotation = orthonormal_steps(gram_sum, rank_cols).astype(jnp.bfloat16)
    product = jnp.dot(moved, rotation[:rank_cols], preferred_element_type=jnp.float32)
    product += jnp.dot(bathed, rotation[rank_cols:], preferred_element_type=jnp.float32)
    return product.astype(jnp.bfloat16)


def solution(mesh):
    placed = (
        P(("row", "col"), None),
        P(("row", "col")),
        P(("row", "col"), None),
        P(("row", "col")),
        P(("row", "col"), None),
        P(),
        P(("row", "col")),
        P(),
    )
    return jax.shard_map(
        shards, mesh=mesh, in_specs=placed, out_specs=P(("row", "col"), None), check_vma=False
    )
```

```python
import functools

import jax
import jax.numpy as jnp
from jax import lax
from jax.experimental import pallas as pl
from jax.experimental.pallas import tpu as pltpu
from jax.sharding import PartitionSpec as P

SWEEPS = 2


time_step = 0.25


def orthonormal_steps(gram, rank_cols):
    def sweep(_, basis):
        image = jnp.dot(gram, basis, precision=lax.Precision.HIGHEST)
        inner = jnp.dot(image.T, image, precision=lax.Precision.HIGHEST)
        factor = jnp.linalg.cholesky(inner)
        return lax.linalg.triangular_solve(
            factor, image, left_side=False, lower=True, transpose_a=True
        )

    return lax.fori_loop(0, SWEEPS, sweep, jnp.eye(2 * rank_cols, rank_cols, dtype=jnp.float32))


def step_kernel(slots, ids_ref, cnt_ref, kind_ref,
                group_hbm, own_ref, ons_ref, cpl_hbm, out_ref, buf, sems, acc, cpl_ref, cpl_sem):
    b = pl.program_id(0)
    last = pl.num_programs(0) - 1
    rank_cols = own_ref.shape[2]

    def fetch(blk, slot):
        for k in range(slots):
            @pl.when(k < cnt_ref[blk])
            def _():
                pltpu.make_async_copy(
                    group_hbm.at[ids_ref[blk * slots + k]], buf.at[slot, k], sems.at[slot, k]
                ).start()

    @pl.when(b == 0)
    def _():
        fetch(0, 0)
        pltpu.make_async_copy(cpl_hbm, cpl_ref, cpl_sem).start()

    @pl.when(b < last)
    def _():
        fetch(b + 1, (b + 1) % 2)

    slot = b % 2
    acc[...] = jnp.zeros_like(acc)
    for k in range(slots):
        @pl.when(k < cnt_ref[b])
        def _():
            pltpu.make_async_copy(group_hbm.at[0], buf.at[slot, k], sems.at[slot, k]).wait()
            t = kind_ref[b * slots + k]
            acc[t] += buf[slot, k].astype(jnp.float32)

    @pl.when(b == 0)
    def _():
        pltpu.make_async_copy(cpl_hbm, cpl_ref, cpl_sem).wait()

    coupled = jnp.dot(cpl_ref[0], acc[0].astype(jnp.bfloat16), preferred_element_type=jnp.float32)
    for t in range(1, cpl_ref.shape[0]):
        coupled += jnp.dot(cpl_ref[t], acc[t].astype(jnp.bfloat16), preferred_element_type=jnp.float32)
    own = own_ref[0]
    wide = own.astype(jnp.float32)
    moved = wide - time_step * (ons_ref[0] * wide + coupled)
    out_ref[0] = moved.astype(out_ref.dtype)


def moved_blocks(group_rows, own_rows, energy, ids, counts, kinds, coupling_blocks):
    blocks, block_rows, rank_cols = own_rows.shape
    slots = ids.shape[0] // blocks
    kinds_n = coupling_blocks.shape[0]
    grid_spec = pltpu.PrefetchScalarGridSpec(
        num_scalar_prefetch=3,
        grid=(blocks,),
        in_specs=[
            pl.BlockSpec(memory_space=pl.ANY),
            pl.BlockSpec((1, block_rows, rank_cols), lambda b, *_: (b, 0, 0)),
            pl.BlockSpec((1, block_rows, 1), lambda b, *_: (b, 0, 0)),
            pl.BlockSpec(memory_space=pl.ANY),
        ],
        out_specs=pl.BlockSpec((1, block_rows, rank_cols), lambda b, *_: (b, 0, 0)),
        scratch_shapes=[
            pltpu.VMEM((2, slots, block_rows, rank_cols), group_rows.dtype),
            pltpu.SemaphoreType.DMA((2, slots)),
            pltpu.VMEM((kinds_n, block_rows, rank_cols), jnp.float32),
            pltpu.VMEM(coupling_blocks.shape, coupling_blocks.dtype),
            pltpu.SemaphoreType.DMA(()),
        ],
    )
    return pl.pallas_call(
        functools.partial(step_kernel, slots),
        grid_spec=grid_spec,
        out_shape=jax.ShapeDtypeStruct((blocks, block_rows, rank_cols), jnp.bfloat16),
        compiler_params=pltpu.CompilerParams(dimension_semantics=("arbitrary",)),
    )(ids, counts, kinds, group_rows, own_rows, energy, coupling_blocks)


def allreduce_kernel(fields, cols, x_ref, o_ref, *scratch):
    stages = len(fields)
    recv_bufs = scratch[:stages]
    send_sems, recv_sems, work = scratch[stages], scratch[stages + 1], scratch[stages + 2]
    me = lax.axis_index("row") * cols + lax.axis_index("col")

    def field(s, r):
        return (me // (1 << s)) % r

    def place(s, r, d):
        other = me + ((field(s, r) + d) % r - field(s, r)) * (1 << s)
        return (other // cols, other % cols)

    barrier = pltpu.get_barrier_semaphore()
    partners = 0
    for s, r in fields:
        for d in range(1, r):
            pl.semaphore_signal(barrier, inc=1, device_id=place(s, r, d), device_id_type=pl.DeviceIdType.MESH)
            partners += 1
    pl.semaphore_wait(barrier, partners)

    base = 0
    size = x_ref.shape[0]
    slot = 0
    for j, (s, r) in enumerate(fields):
        part = size // r
        f = field(s, r)
        src = x_ref if j == 0 else work
        copies = []
        for d in range(1, r):
            give = pl.multiple_of(base + ((f + d) % r) * part, 8)
            copy = pltpu.make_async_remote_copy(
                src_ref=src.at[pl.ds(give, part)],
                dst_ref=recv_bufs[j].at[d - 1],
                send_sem=send_sems.at[slot],
                recv_sem=recv_sems.at[slot],
                device_id=place(s, r, d),
                device_id_type=pl.DeviceIdType.MESH,
            )
            copy.start()
            copies.append(copy)
            slot += 1
        for copy in copies:
            copy.wait()
        keep = pl.multiple_of(base + f * part, 8)
        total = src[pl.ds(keep, part)]
        for d in range(1, r):
            total = total + recv_bufs[j][d - 1]
        work[pl.ds(keep, part)] = total
        base, size = keep, part
    o_ref[pl.ds(base, size)] = work[pl.ds(base, size)]
    for j in reversed(range(stages)):
        s, r = fields[j]
        block = o_ref.at[pl.ds(base, size)]
        copies = []
        for d in range(1, r):
            copy = pltpu.make_async_remote_copy(
                src_ref=block,
                dst_ref=block,
                send_sem=send_sems.at[slot],
                recv_sem=recv_sems.at[slot],
                device_id=place(s, r, d),
                device_id_type=pl.DeviceIdType.MESH,
            )
            copy.start()
            copies.append(copy)
            slot += 1
        for copy in copies:
            copy.wait()
        base = pl.multiple_of(base - field(s, r) * size, 8)
        size = size * r


def kernel_sum(local, fields, cols, channel):
    lanes = 128
    flat = local.reshape(-1, lanes)
    rows = flat.shape[0]
    scratch = []
    left = rows
    for s, r in fields:
        left //= r
        scratch.append(pltpu.VMEM((r - 1, left, lanes), jnp.float32))
    copies = 2 * sum(r - 1 for _, r in fields)
    scratch += [pltpu.SemaphoreType.DMA((copies,)), pltpu.SemaphoreType.DMA((copies,))]
    scratch += [pltpu.VMEM(flat.shape, jnp.float32)]
    total = pl.pallas_call(
        functools.partial(allreduce_kernel, tuple(fields), cols),
        out_shape=jax.ShapeDtypeStruct(flat.shape, flat.dtype),
        in_specs=[pl.BlockSpec(memory_space=pltpu.VMEM)],
        out_specs=pl.BlockSpec(memory_space=pltpu.VMEM),
        scratch_shapes=scratch,
        compiler_params=pltpu.CompilerParams(collective_id=channel, has_side_effects=True),
    )(flat)
    return total.reshape(local.shape)


def shards(
    density_factor,
    onsite,
    neighbour_ids,
    neighbour_count,
    coupling_type,
    coupling_blocks,
    bath_pattern,
    bath_blocks,
):
    blocks, slots = neighbour_ids.shape
    block_rows = coupling_blocks.shape[1]
    rank_cols = density_factor.shape[1]
    col_count = lax.axis_size("col")
    group_blocks = col_count * blocks
    row_place = lax.axis_index("row")
    in_group = jnp.clip(neighbour_ids - row_place * group_blocks, 0, group_blocks - 1)
    counts = jnp.clip(neighbour_count, 1, slots)
    kinds = jnp.clip(coupling_type, 0, coupling_blocks.shape[0] - 1)
    bath_kind = jnp.clip(bath_pattern, 0, bath_blocks.shape[0] - 1)
    own_rows = density_factor.reshape(blocks, block_rows, rank_cols)
    bathed = jnp.einsum(
        "bij,bjr->bir", bath_blocks[bath_kind], own_rows, preferred_element_type=jnp.float32
    ).astype(jnp.bfloat16).reshape(blocks * block_rows, rank_cols)
    contract_rows = (((0,), (0,)), ((), ()))
    bath_gram = lax.dot_general(bathed, bathed, contract_rows, preferred_element_type=jnp.float32)
    devices = lax.axis_size("row") * col_count
    stage_bits = devices.bit_length() - 1
    if stage_bits == 7:
        fields = [(4, 2), (0, 16), (5, 4)]
    else:
        fields = [(s, 2) for s in range(stage_bits)]
    bath_flat = bath_gram.reshape(-1, 128)
    bath_flat = jnp.concatenate([bath_flat, jnp.zeros_like(bath_flat)], axis=0)
    early_fields = [(4, 2), (5, 4), (0, 16)] if stage_bits == 7 else fields
    bath_sum = kernel_sum(bath_flat, early_fields, col_count, 1)[: bath_flat.shape[0] // 2]
    bath_sum = bath_sum.reshape(bath_gram.shape)
    gathered = lax.all_gather(density_factor, "col", axis=0, tiled=True)
    group_rows = gathered.reshape(group_blocks, block_rows, rank_cols)
    energy = onsite.reshape(blocks, block_rows, 1)
    moved = moved_blocks(
        group_rows, own_rows, energy, in_group.reshape(-1), counts, kinds.reshape(-1), coupling_blocks,
    ).reshape(blocks * block_rows, rank_cols)
    moved_gram = lax.dot_general(moved, moved, contract_rows, preferred_element_type=jnp.float32)
    cross_gram = lax.dot_general(moved, bathed, contract_rows, preferred_element_type=jnp.float32)
    upper = kernel_sum(jnp.concatenate([moved_gram, cross_gram], axis=0), fields, col_count, 0)
    moved_sum, cross_sum = upper[:rank_cols], upper[rank_cols:]
    gram_sum = jnp.concatenate(
        [
            jnp.concatenate([moved_sum, cross_sum], axis=1),
            jnp.concatenate([cross_sum.T, bath_sum], axis=1),
        ],
        axis=0,
    )
    rotation = orthonormal_steps(gram_sum, rank_cols).astype(jnp.bfloat16)
    product = jnp.dot(moved, rotation[:rank_cols], preferred_element_type=jnp.float32)
    product += jnp.dot(bathed, rotation[rank_cols:], preferred_element_type=jnp.float32)
    return product.astype(jnp.bfloat16)


def solution(mesh):
    placed = (
        P(("row", "col"), None),
        P(("row", "col")),
        P(("row", "col"), None),
        P(("row", "col")),
        P(("row", "col"), None),
        P(),
        P(("row", "col")),
        P(),
    )
    return jax.shard_map(
        shards, mesh=mesh, in_specs=placed, out_specs=P(("row", "col"), None), check_vma=False
    )
```

```python
import functools

import jax
import jax.numpy as jnp
from jax import lax
from jax.experimental import pallas as pl
from jax.experimental.pallas import tpu as pltpu
from jax.sharding import PartitionSpec as P

SWEEPS = 2


time_step = 0.25


def orthonormal_steps(gram, rank_cols):
    def sweep(_, basis):
        image = jnp.dot(gram, basis, precision=lax.Precision.HIGHEST)
        inner = jnp.dot(image.T, image, precision=lax.Precision.HIGHEST)
        factor = jnp.linalg.cholesky(inner)
        return lax.linalg.triangular_solve(
            factor, image, left_side=False, lower=True, transpose_a=True
        )

    return lax.fori_loop(0, SWEEPS, sweep, jnp.eye(2 * rank_cols, rank_cols, dtype=jnp.float32))


def step_kernel(slots, ids_ref, cnt_ref, kind_ref,
                group_hbm, own_ref, ons_ref, cpl_hbm, bth_ref, out_ref, buf, sems, acc, cpl_ref, cpl_sem):
    b = pl.program_id(0)
    last = pl.num_programs(0) - 1
    rank_cols = own_ref.shape[2]

    def fetch(blk, slot):
        for k in range(slots):
            @pl.when(k < cnt_ref[blk])
            def _():
                pltpu.make_async_copy(
                    group_hbm.at[ids_ref[blk * slots + k]], buf.at[slot, k], sems.at[slot, k]
                ).start()

    @pl.when(b == 0)
    def _():
        fetch(0, 0)
        pltpu.make_async_copy(cpl_hbm, cpl_ref, cpl_sem).start()

    @pl.when(b < last)
    def _():
        fetch(b + 1, (b + 1) % 2)

    slot = b % 2
    acc[...] = jnp.zeros_like(acc)
    for k in range(slots):
        @pl.when(k < cnt_ref[b])
        def _():
            pltpu.make_async_copy(group_hbm.at[0], buf.at[slot, k], sems.at[slot, k]).wait()
            t = kind_ref[b * slots + k]
            acc[t] += buf[slot, k].astype(jnp.float32)

    @pl.when(b == 0)
    def _():
        pltpu.make_async_copy(cpl_hbm, cpl_ref, cpl_sem).wait()

    coupled = jnp.dot(cpl_ref[0], acc[0].astype(jnp.bfloat16), preferred_element_type=jnp.float32)
    for t in range(1, cpl_ref.shape[0]):
        coupled += jnp.dot(cpl_ref[t], acc[t].astype(jnp.bfloat16), preferred_element_type=jnp.float32)
    own = own_ref[0]
    wide = own.astype(jnp.float32)
    moved = wide - time_step * (ons_ref[0] * wide + coupled)
    out_ref[0, :, :rank_cols] = moved.astype(out_ref.dtype)
    out_ref[0, :, rank_cols:] = bth_ref[0]


def moved_blocks(group_rows, own_rows, energy, ids, counts, kinds, coupling_blocks, bathed):
    blocks, block_rows, rank_cols = own_rows.shape
    slots = ids.shape[0] // blocks
    kinds_n = coupling_blocks.shape[0]
    grid_spec = pltpu.PrefetchScalarGridSpec(
        num_scalar_prefetch=3,
        grid=(blocks,),
        in_specs=[
            pl.BlockSpec(memory_space=pl.ANY),
            pl.BlockSpec((1, block_rows, rank_cols), lambda b, *_: (b, 0, 0)),
            pl.BlockSpec((1, block_rows, 1), lambda b, *_: (b, 0, 0)),
            pl.BlockSpec(memory_space=pl.ANY),
            pl.BlockSpec((1, block_rows, rank_cols), lambda b, *_: (b, 0, 0)),
        ],
        out_specs=pl.BlockSpec((1, block_rows, 2 * rank_cols), lambda b, *_: (b, 0, 0)),
        scratch_shapes=[
            pltpu.VMEM((2, slots, block_rows, rank_cols), group_rows.dtype),
            pltpu.SemaphoreType.DMA((2, slots)),
            pltpu.VMEM((kinds_n, block_rows, rank_cols), jnp.float32),
            pltpu.VMEM(coupling_blocks.shape, coupling_blocks.dtype),
            pltpu.SemaphoreType.DMA(()),
        ],
    )
    return pl.pallas_call(
        functools.partial(step_kernel, slots),
        grid_spec=grid_spec,
        out_shape=jax.ShapeDtypeStruct((blocks, block_rows, 2 * rank_cols), jnp.bfloat16),
        compiler_params=pltpu.CompilerParams(dimension_semantics=("arbitrary",)),
    )(ids, counts, kinds, group_rows, own_rows, energy, coupling_blocks, bathed)


def allreduce_kernel(fields, cols, x_ref, o_ref, *scratch):
    stages = len(fields)
    recv_bufs = scratch[:stages]
    send_sems, recv_sems, work = scratch[stages], scratch[stages + 1], scratch[stages + 2]
    me = lax.axis_index("row") * cols + lax.axis_index("col")

    def field(s, r):
        return (me // (1 << s)) % r

    def place(s, r, d):
        other = me + ((field(s, r) + d) % r - field(s, r)) * (1 << s)
        return (other // cols, other % cols)

    barrier = pltpu.get_barrier_semaphore()
    partners = 0
    for s, r in fields:
        for d in range(1, r):
            pl.semaphore_signal(barrier, inc=1, device_id=place(s, r, d), device_id_type=pl.DeviceIdType.MESH)
            partners += 1
    pl.semaphore_wait(barrier, partners)

    base = 0
    size = x_ref.shape[0]
    slot = 0
    for j, (s, r) in enumerate(fields):
        part = size // r
        f = field(s, r)
        src = x_ref if j == 0 else work
        copies = []
        for d in range(1, r):
            give = pl.multiple_of(base + ((f + d) % r) * part, 8)
            copy = pltpu.make_async_remote_copy(
                src_ref=src.at[pl.ds(give, part)],
                dst_ref=recv_bufs[j].at[d - 1],
                send_sem=send_sems.at[slot],
                recv_sem=recv_sems.at[slot],
                device_id=place(s, r, d),
                device_id_type=pl.DeviceIdType.MESH,
            )
            copy.start()
            copies.append(copy)
            slot += 1
        for copy in copies:
            copy.wait()
        keep = pl.multiple_of(base + f * part, 8)
        total = src[pl.ds(keep, part)]
        for d in range(1, r):
            total = total + recv_bufs[j][d - 1]
        work[pl.ds(keep, part)] = total
        base, size = keep, part
    o_ref[pl.ds(base, size)] = work[pl.ds(base, size)]
    for j in reversed(range(stages)):
        s, r = fields[j]
        block = o_ref.at[pl.ds(base, size)]
        copies = []
        for d in range(1, r):
            copy = pltpu.make_async_remote_copy(
                src_ref=block,
                dst_ref=block,
                send_sem=send_sems.at[slot],
                recv_sem=recv_sems.at[slot],
                device_id=place(s, r, d),
                device_id_type=pl.DeviceIdType.MESH,
            )
            copy.start()
            copies.append(copy)
            slot += 1
        for copy in copies:
            copy.wait()
        base = pl.multiple_of(base - field(s, r) * size, 8)
        size = size * r


def kernel_sum(local, fields, cols, channel):
    lanes = 128
    flat = local.reshape(-1, lanes)
    rows = flat.shape[0]
    scratch = []
    left = rows
    for s, r in fields:
        left //= r
        scratch.append(pltpu.VMEM((r - 1, left, lanes), jnp.float32))
    copies = 2 * sum(r - 1 for _, r in fields)
    scratch += [pltpu.SemaphoreType.DMA((copies,)), pltpu.SemaphoreType.DMA((copies,))]
    scratch += [pltpu.VMEM(flat.shape, jnp.float32)]
    total = pl.pallas_call(
        functools.partial(allreduce_kernel, tuple(fields), cols),
        out_shape=jax.ShapeDtypeStruct(flat.shape, flat.dtype),
        in_specs=[pl.BlockSpec(memory_space=pltpu.VMEM)],
        out_specs=pl.BlockSpec(memory_space=pltpu.VMEM),
        scratch_shapes=scratch,
        compiler_params=pltpu.CompilerParams(collective_id=channel, has_side_effects=True),
    )(flat)
    return total.reshape(local.shape)


def shards(
    density_factor,
    onsite,
    neighbour_ids,
    neighbour_count,
    coupling_type,
    coupling_blocks,
    bath_pattern,
    bath_blocks,
):
    blocks, slots = neighbour_ids.shape
    block_rows = coupling_blocks.shape[1]
    rank_cols = density_factor.shape[1]
    col_count = lax.axis_size("col")
    group_blocks = col_count * blocks
    row_place = lax.axis_index("row")
    in_group = jnp.clip(neighbour_ids - row_place * group_blocks, 0, group_blocks - 1)
    counts = jnp.clip(neighbour_count, 1, slots)
    kinds = jnp.clip(coupling_type, 0, coupling_blocks.shape[0] - 1)
    bath_kind = jnp.clip(bath_pattern, 0, bath_blocks.shape[0] - 1)
    own_rows = density_factor.reshape(blocks, block_rows, rank_cols)
    bathed = jnp.einsum(
        "bij,bjr->bir", bath_blocks[bath_kind], own_rows, preferred_element_type=jnp.float32
    ).astype(jnp.bfloat16).reshape(blocks * block_rows, rank_cols)
    contract_rows = (((0,), (0,)), ((), ()))
    bath_gram = lax.dot_general(bathed, bathed, contract_rows, preferred_element_type=jnp.float32)
    devices = lax.axis_size("row") * col_count
    stage_bits = devices.bit_length() - 1
    if stage_bits == 7:
        fields = [(4, 2), (0, 16), (5, 4)]
    else:
        fields = [(s, 2) for s in range(stage_bits)]
    bath_flat = bath_gram.reshape(-1, 128)
    bath_flat = jnp.concatenate([bath_flat, jnp.zeros_like(bath_flat)], axis=0)
    early_fields = [(4, 2), (5, 4), (0, 16)] if stage_bits == 7 else fields
    bath_sum = kernel_sum(bath_flat, early_fields, col_count, 1)[: bath_flat.shape[0] // 2]
    bath_sum = bath_sum.reshape(bath_gram.shape)
    gathered = lax.all_gather(density_factor, "col", axis=0, tiled=True)
    group_rows = gathered.reshape(group_blocks, block_rows, rank_cols)
    energy = onsite.reshape(blocks, block_rows, 1)
    stacked = moved_blocks(
        group_rows, own_rows, energy, in_group.reshape(-1), counts, kinds.reshape(-1), coupling_blocks,
        bathed.reshape(blocks, block_rows, rank_cols),
    ).reshape(blocks * block_rows, 2 * rank_cols)
    top = lax.dot_general(stacked[:, :rank_cols], stacked, contract_rows, preferred_element_type=jnp.float32)
    upper = kernel_sum(top, fields, col_count, 0)
    moved_sum, cross_sum = upper[:, :rank_cols], upper[:, rank_cols:]
    gram_sum = jnp.concatenate(
        [
            jnp.concatenate([moved_sum, cross_sum], axis=1),
            jnp.concatenate([cross_sum.T, bath_sum], axis=1),
        ],
        axis=0,
    )
    rotation = orthonormal_steps(gram_sum, rank_cols).astype(jnp.bfloat16)
    return jnp.dot(stacked, rotation, preferred_element_type=jnp.float32).astype(jnp.bfloat16)


def solution(mesh):
    placed = (
        P(("row", "col"), None),
        P(("row", "col")),
        P(("row", "col"), None),
        P(("row", "col")),
        P(("row", "col"), None),
        P(),
        P(("row", "col")),
        P(),
    )
    return jax.shard_map(
        shards, mesh=mesh, in_specs=placed, out_specs=P(("row", "col"), None), check_vma=False
    )
```
